768 devices in a mesh: curve: 96 (over z, y), near: 8 (over x, core).
Axes of the slice: x: 4, y: 8, z: 12, core: 2. Of those that a mesh axis runs over, the one named last changes fastest.
Arguments:
- primitive: float32 [6, 32, 294912], P(None, 'near', 'curve'), may hold values from -2 to 2, as said below
- conductivity: float32 [32, 294912], P('near', 'curve'), may hold values from 0.05 to 0.5
- new_owner: int32 [288], P('curve'), may hold values from 0 to 95, as said below
Outputs:
- regridded: float32 [96, 6, 32, 4096], P('curve', None, 'near')
The draws below stay inside these ranges and needn't reach their ends.
Inputs may be any that keep to these rules, and one draw needn't show every extreme that they name: `primitive`: fields in order: density and pressure within 0.5 to 2, three velocity components within -2 to 2, tracer concentration within 0 to 1. `new_owner`: before the regrid box column b lies on curve segment b // 3. Its new owner is that segment, except that the first box column of a segment c >= 1 may go to c - 1. Some segment ends with 4 box columns and some with 2.
All inputs are finite; a program needn't handle non-finite values.
Results may differ from the reference program's by a relative error of at most 0.0003.
Values sent between devices are 32-bit elements; how exact they have to be, the bound alone decides.
A program may use at most 32 MiB of HBM per device.

```python
import math
import jax
import jax.numpy as jnp
from jax import lax

BW = 32
BOX_DEV = 3
CAP = 4
XBOXES = 288
NZ_CELLS = 32
N_CURVE = 96


def draw_primitive(key, part):
    keys = jax.random.split(key, 4)
    shape = (NZ_CELLS, XBOXES * BW * BW)
    specific_weight_field = jnp.exp(jax.random.uniform(keys[0], shape, jnp.float32, jnp.log(0.5), jnp.log(2.0)))
    normal_stress_field = jnp.exp(jax.random.uniform(keys[1], shape, jnp.float32, jnp.log(0.5), jnp.log(2.0)))
    velocity = jnp.clip(0.5 * jax.random.normal(keys[2], (3,) + shape, jnp.float32), -2.0, 2.0)
    tracer = jax.random.uniform(keys[3], shape, jnp.float32, 0.0, 1.0)
    return jnp.concatenate([specific_weight_field[None], velocity, normal_stress_field[None], tracer[None]], axis=0)


def draw_new_owner(key, part):
    columns = jnp.arange(XBOXES, dtype=jnp.int32)
    segment_of = columns // BOX_DEV
    slot_of = columns % BOX_DEV
    segments = jnp.arange(N_CURVE, dtype=jnp.int32)
    leaving = jax.random.randint(key, (N_CURVE,), 0, 2).astype(jnp.int32)
    leaving = jnp.where(segments <= 1, 0, leaving)
    leaving = jnp.where(segments == 2, 1, leaving)
    leaving = jnp.where(segments == 3, 0, leaving)
    shifted = leaving[segment_of] * (slot_of == 0).astype(jnp.int32)
    return (segment_of - shifted).astype(jnp.int32)


def block_levels(stream_key, shape, cuts, smallest, largest):
    gain, own = 1.0, jax.random.fold_in(stream_key, 6)
    for axis_at, blocks in cuts:
        heights = jnp.exp(jax.random.uniform(jax.random.fold_in(own, axis_at), (blocks,), jnp.float32, smallest / len(cuts), largest / len(cuts)))
        gain = gain * jnp.repeat(heights, shape[axis_at] // blocks).reshape([-1 if axis == axis_at else 1 for axis in range(len(shape))])
    return gain


def setup_inputs(seed: int = 0) -> dict:
    streams_of = jax.random.split(jax.random.key(seed), 4)
    return {
        "primitive": draw_primitive(jax.random.fold_in(streams_of[3], 71), 0),
        "conductivity": jnp.clip(jnp.exp(math.log(0.5) - 2.3025851 * jax.random.uniform(streams_of[1], (NZ_CELLS, XBOXES * BW * BW), jnp.float32) ** block_levels(streams_of[1], (NZ_CELLS, XBOXES * BW * BW), ((0, 8), (1, 96)), -0.2, 0.2)), 0.05, 0.5),
        "new_owner": draw_new_owner(jax.random.fold_in(streams_of[3], 71), 0),
    }


GAMMA = 1.4
COURANT = 0.8

def to_conserved(prim):
    specific_weight_field = prim[0]
    velocity = prim[1:4]
    normal_stress_field = prim[4]
    momentum = specific_weight_field[None] * velocity
    energy = normal_stress_field / (GAMMA - 1.0) + 0.5 * specific_weight_field * lax.optimization_barrier(jnp.sum(velocity * velocity, axis=0))
    tracer = specific_weight_field * prim[5]
    return jnp.concatenate([specific_weight_field[None], momentum, energy[None], tracer[None]], axis=0)

def wave_bound(prim):
    sound = jnp.sqrt(GAMMA * prim[4] / prim[0])
    return jnp.abs(prim[1]) + jnp.abs(prim[2]) + jnp.abs(prim[3]) + 3.0 * sound

def roll_upper(values, ypos, ghost_layer_depth):
    return jnp.where(ypos == ghost_layer_depth - 1, jnp.roll(values, ghost_layer_depth - 1, axis=-1), jnp.roll(values, -1, axis=-1))

def roll_lower(values, ypos, ghost_layer_depth):
    return jnp.where(ypos == 0, jnp.roll(values, 1 - ghost_layer_depth, axis=-1), jnp.roll(values, 1, axis=-1))

def face_flux(lower_u, upper_u, lower_f, upper_f, lower_s, upper_s, lower_k, upper_k, lower_t, upper_t):
    flux = 0.5 * (lower_f + upper_f) - 0.5 * jnp.maximum(lower_s, upper_s)[None] * (upper_u - lower_u)
    heat = 0.5 * (lower_k + upper_k) * (upper_t - lower_t)
    return flux.at[4].add(-heat)

def compute_rate(extended, ext_kappa, ghost_layer_depth):
    specific_weight_field = extended[0]
    velocity = extended[1:4] / specific_weight_field[None]
    kinetic = 0.5 * lax.optimization_barrier(jnp.sum(extended[1:4] * velocity, axis=0))
    normal_stress_field = (GAMMA - 1.0) * (extended[4] - kinetic)
    sound = jnp.sqrt(GAMMA * normal_stress_field / specific_weight_field)
    thermal_state_kelvin = normal_stress_field / specific_weight_field

    def physical(direction):
        speed_dir = velocity[direction]
        fluxes = extended * speed_dir[None]
        fluxes = fluxes.at[1 + direction].add(normal_stress_field)
        fluxes = fluxes.at[4].add(normal_stress_field * speed_dir)
        return (fluxes, jnp.abs(speed_dir) + sound)
    fluxes, signal = physical(0)
    rows_u = extended[:, 1:-1]
    rows_f = fluxes[:, 1:-1]
    rows_s = signal[1:-1]
    rows_k = ext_kappa[1:-1]
    horizontal_line_number = thermal_state_kelvin[1:-1]
    faces = face_flux(rows_u[..., :-ghost_layer_depth], rows_u[..., ghost_layer_depth:], rows_f[..., :-ghost_layer_depth], rows_f[..., ghost_layer_depth:], rows_s[..., :-ghost_layer_depth], rows_s[..., ghost_layer_depth:], rows_k[..., :-ghost_layer_depth], rows_k[..., ghost_layer_depth:], horizontal_line_number[..., :-ghost_layer_depth], horizontal_line_number[..., ghost_layer_depth:])
    total = faces[..., ghost_layer_depth:] - faces[..., :-ghost_layer_depth]
    fluxes, signal = physical(2)
    cols_u = extended[..., ghost_layer_depth:-ghost_layer_depth]
    cols_f = fluxes[..., ghost_layer_depth:-ghost_layer_depth]
    cols_s = signal[..., ghost_layer_depth:-ghost_layer_depth]
    cols_k = ext_kappa[..., ghost_layer_depth:-ghost_layer_depth]
    vertical_count_grid = thermal_state_kelvin[..., ghost_layer_depth:-ghost_layer_depth]
    faces = face_flux(cols_u[:, :-1], cols_u[:, 1:], cols_f[:, :-1], cols_f[:, 1:], cols_s[:-1], cols_s[1:], cols_k[:-1], cols_k[1:], vertical_count_grid[:-1], vertical_count_grid[1:])
    total = total + faces[:, 1:] - faces[:, :-1]
    fluxes, signal = physical(1)
    inner_u = extended[:, 1:-1, ghost_layer_depth:-ghost_layer_depth]
    inner_f = fluxes[:, 1:-1, ghost_layer_depth:-ghost_layer_depth]
    inner_s = signal[1:-1, ghost_layer_depth:-ghost_layer_depth]
    inner_k = ext_kappa[1:-1, ghost_layer_depth:-ghost_layer_depth]
    core_cell_number = thermal_state_kelvin[1:-1, ghost_layer_depth:-ghost_layer_depth]
    ypos = jnp.arange(inner_u.shape[-1]) % ghost_layer_depth
    faces = face_flux(inner_u, roll_upper(inner_u, ypos, ghost_layer_depth), inner_f, roll_upper(inner_f, ypos, ghost_layer_depth), inner_s, roll_upper(inner_s, ypos, ghost_layer_depth), inner_k, roll_upper(inner_k, ypos, ghost_layer_depth), core_cell_number, roll_upper(core_cell_number, ypos, ghost_layer_depth))
    total = total + faces - roll_lower(faces, ypos, ghost_layer_depth)
    return -total

def chain_rate(state, kappa):
    ghost_layer_depth = BW
    box_cells = BW * BW
    joined = jnp.concatenate([state, kappa[None]], axis=0)
    length = joined.shape[-1]
    box_total = length // box_cells

    def one_box(index):
        start = (index * box_cells).astype(jnp.int32)
        slab = lax.dynamic_slice_in_dim(joined, start, box_cells, 2)
        before = lax.dynamic_slice_in_dim(joined, jnp.maximum(start - ghost_layer_depth, 0).astype(jnp.int32), ghost_layer_depth, 2)
        after = lax.dynamic_slice_in_dim(joined, jnp.minimum(start + box_cells, length - ghost_layer_depth).astype(jnp.int32), ghost_layer_depth, 2)
        before = jnp.where(index == 0, slab[..., :ghost_layer_depth], before)
        after = jnp.where(index == box_total - 1, slab[..., -ghost_layer_depth:], after)
        broad = jnp.concatenate([before, slab, after], axis=2)
        framed = jnp.concatenate([broad[:, -1:], broad, broad[:, :1]], axis=1)
        return compute_rate(framed[:6], framed[6], ghost_layer_depth)
    rates = lax.map(one_box, jnp.arange(box_total, dtype=jnp.int32))
    rates = jnp.transpose(rates, (1, 2, 0, 3))
    return rates.reshape(state.shape)

def reference(primitive, conductivity, new_owner):
    top_speed = jnp.max(wave_bound(primitive))
    top_kappa = jnp.max(conductivity)
    time_step = COURANT / (top_speed + 6.0 * top_kappa)
    state = to_conserved(primitive)
    half = state + time_step * chain_rate(state, conductivity)
    final = 0.5 * state + 0.5 * (half + time_step * chain_rate(half, conductivity))
    counts = jax.ops.segment_sum(jnp.ones_like(new_owner), new_owner, num_segments=N_CURVE).astype(jnp.int32)
    starts = (jnp.cumsum(counts) - counts).astype(jnp.int32)
    box_cells = BW * BW

    def one_segment(segment):
        pieces = []
        for slot in range(CAP):
            column = jnp.minimum(starts[segment] + slot, XBOXES - 1).astype(jnp.int32)
            piece = lax.dynamic_slice_in_dim(final, (column * box_cells).astype(jnp.int32), box_cells, 2)
            pieces.append(jnp.where(slot < counts[segment], piece, 0.0))
        return jnp.concatenate(pieces, axis=2)
    return lax.map(one_segment, jnp.arange(N_CURVE, dtype=jnp.int32))
```

```python
import functools

import jax
import jax.numpy as jnp
from jax import lax
from jax.experimental import pallas as pl
from jax.experimental.pallas import tpu as pltpu
from jax.sharding import PartitionSpec as P

BW = 32
BOXES = 3
DEPTH = 4
LANES = 128
OWN = 24
ROWS = 40
NEXT = 40
PREV = 8
Y_CHIPS = 8
MESH = pl.DeviceIdType.MESH
F32 = jnp.float32


def lane_of(shape):
    return lax.broadcasted_iota(jnp.int32, shape, len(shape) - 1)


def row_of(shape):
    return lax.broadcasted_iota(jnp.int32, shape, 0)


def upper_y(v, ypos):
    return jnp.where(ypos == BW - 1, pltpu.roll(v, BW - 1, 1), pltpu.roll(v, LANES - 1, 1))


def lower_y(v, ypos):
    return jnp.where(ypos == 0, pltpu.roll(v, LANES - BW + 1, 1), pltpu.roll(v, 1, 1))


def upper_x(v, lane):
    above = pltpu.roll(v, v.shape[0] - 1, 0)
    return pltpu.roll(jnp.where(lane < BW, above, v), LANES - BW, 1)


def lower_x(v, lane):
    below = pltpu.roll(v, 1, 0)
    return pltpu.roll(jnp.where(lane >= LANES - BW, below, v), BW, 1)


def derive(cons):
    r, mx, my, mz, energy = cons[:5]
    inv = 1.0 / r
    vx, vy, vz = mx * inv, my * inv, mz * inv
    pressure = 0.4 * (energy - 0.5 * (mx * vx + my * vy + mz * vz))
    temp = pressure * inv
    return 0.5 * vx, 0.5 * vy, 0.5 * vz, 0.5 * jnp.sqrt(1.4 * temp), 0.5 * pressure, temp


def face(lo, hi, k):
    lu, ld, lc = lo
    hu, hd, hc = hi
    lw, hw = ld[k], hd[k]
    top = jnp.maximum(jnp.abs(lw) + ld[3], jnp.abs(hw) + hd[3])
    lf, hf = lw + top, hw - top
    flux = [a * lf + b * hf for a, b in zip(lu, hu)]
    flux[1 + k] = flux[1 + k] + (ld[4] + hd[4])
    work = ld[4] * lw + hd[4] * hw
    flux[4] = flux[4] + (work + work) - (lc + hc) * (hd[5] - ld[5])
    return flux


def mapped(cell, fn):
    u, d, c = cell
    return [fn(a) for a in u], [fn(a) for a in d], fn(c)


def plane_rate(get, z):
    mid = get(z)
    shape = mid[2].shape
    lane = lane_of(shape)
    ypos = lane % BW
    flux = face(mid, mapped(mid, lambda v: upper_x(v, lane)), 0)
    total = [lower_x(f, lane) - f for f in flux]
    flux = face(mid, mapped(mid, lambda v: upper_y(v, ypos)), 1)
    total = [t + (lower_y(f, ypos) - f) for t, f in zip(total, flux)]
    flux = face(mid, get(z + 1), 2)
    total = [t - f for t, f in zip(total, flux)]
    flux = face(get(z - 1), mid, 2)
    return [t + f for t, f in zip(total, flux)]


def spread(ref, f, row):
    return jnp.broadcast_to(ref[f, row : row + 1], (8, LANES))


def conserved(prim):
    r, vx, vy, vz, p, s = prim
    energy = p * 2.5 + 0.5 * r * (vx * vx + vy * vy + vz * vz)
    return r, r * vx, r * vy, r * vz, energy, r * s


def exchange_kernel(
    n_curve, n_near,
    prim_hbm, cond_hbm, owner_hbm,
    u_out, rate_out, top_out, flag_out,
    raw, from_next, from_prev, ext, der, low_planes, high_planes,
    sent, got_near, got_y, got_z, flag_sent, flag_got, owner,
    load_sem, near_send, near_recv, y_send, y_recv, z_send, z_recv, halo_send, halo_recv,
):
    n_y = Y_CHIPS
    n_z = n_curve // n_y
    curve, near = lax.axis_index("curve"), lax.axis_index("near")
    at_y, at_z = curve % n_y, curve // n_y
    loads = [
        pltpu.make_async_copy(prim_hbm, raw.at[pl.ds(0, 6)], load_sem.at[0]),
        pltpu.make_async_copy(cond_hbm, raw.at[6], load_sem.at[1]),
        pltpu.make_async_copy(owner_hbm, owner, load_sem.at[2]),
    ]
    for copy in loads:
        copy.start()

    def far_first(n):
        return sorted(range(1, n), key=lambda j: -min(j, n - j))

    def near_at(j):
        return (curve, (near + j) % n_near)

    def y_at(j):
        return (at_z * n_y + (at_y + j) % n_y, near)

    def z_at(j):
        return (((at_z + j) % n_z) * n_y + at_y, near)

    before, after = ((curve + n_curve - 1) % n_curve, near), ((curve + 1) % n_curve, near)
    partners = [near_at(j) for j in far_first(n_near)] + [y_at(j) for j in far_first(n_y)]
    partners += [z_at(j) for j in far_first(n_z)] + [before, after]
    barrier = pltpu.get_barrier_semaphore()
    for device in partners:
        pl.semaphore_signal(barrier, inc=1, device_id=device, device_id_type=MESH)

    for copy in loads:
        copy.wait()
    speed, cond = None, None
    for i in range(0, raw.shape[1], 8):
        r, vx, vy, vz, p = (raw[f, i : i + 8] for f in range(5))
        here = jnp.abs(vx) + jnp.abs(vy) + jnp.abs(vz) + 3.0 * jnp.sqrt(1.4 * p / r)
        k = raw[6, i : i + 8]
        speed = here if speed is None else jnp.maximum(speed, here)
        cond = k if cond is None else jnp.maximum(cond, k)
    lane8 = lane_of((8, LANES))
    both = jnp.where(
        lane8 < LANES // 2,
        jnp.maximum(speed, pltpu.roll(speed, LANES // 2, 1)),
        jnp.maximum(cond, pltpu.roll(cond, LANES // 2, 1)),
    )
    best = jnp.max(both, axis=0, keepdims=True)
    sent[0] = best
    leaving = jnp.where(owner[0] != curve, 1.0, 0.0).astype(F32)
    flag_sent[...] = jnp.full(flag_sent.shape, leaving, F32)

    pl.semaphore_wait(barrier, len(partners))

    def exchange(stage, got, at, n, send_sem, recv_sem):
        copies = {}
        for j in far_first(n):
            copies[j] = pltpu.make_async_remote_copy(
                src_ref=sent.at[stage], dst_ref=got.at[j - 1], send_sem=send_sem.at[j - 1],
                recv_sem=recv_sem.at[j - 1], device_id=at(j), device_id_type=MESH,
            )
            copies[j].start()
        return [copies[j] for j in range(1, n)]

    def gathered(copies, got, value):
        for copy in copies:
            copy.wait_recv()
        rows = [value] + [got[i] for i in range(len(copies))]
        while len(rows) > 1:
            rows = [jnp.maximum(*rows[i : i + 2]) if i + 1 < len(rows) else rows[i] for i in range(0, len(rows), 2)]
        return rows[0]

    def halo(i, src, dst, device):
        copy = pltpu.make_async_remote_copy(
            src_ref=src, dst_ref=dst, send_sem=halo_send.at[i], recv_sem=halo_recv.at[i],
            device_id=device, device_id_type=MESH,
        )
        copy.start()
        return copy

    near_copies = exchange(0, got_near, near_at, n_near, near_send, near_recv)
    curve_copies = [
        halo(0, raw.at[:, pl.ds(0, NEXT)], from_next, before),
        halo(1, raw.at[:, pl.ds(raw.shape[1] - PREV, PREV)], from_prev, after),
        halo(2, flag_sent, flag_got, before),
    ]

    for z in range(DEPTH):
        for i in range(OWN // 8):
            rows = pl.ds(i * 8 * DEPTH + z, 8, stride=DEPTH)
            for f, value in enumerate(conserved([raw[f, rows] for f in range(6)])):
                ext[f, 2 + z, i * 8 : i * 8 + 8] = value
            ext[6, 2 + z, i * 8 : i * 8 + 8] = 0.5 * raw[6, rows]

    best = gathered(near_copies, got_near, best)
    sent[1] = best
    y_copies = exchange(1, got_y, y_at, n_y, y_send, y_recv)

    first, last = curve == 0, curve == n_curve - 1
    row8 = row_of((8, LANES))
    for copy in curve_copies:
        copy.wait_recv()
    for z in range(DEPTH):
        fourth, sides = [], []
        for f in range(7):
            v = from_next[f, pl.ds(z, 8, stride=DEPTH)]
            edge = pltpu.roll(spread(raw, f, (OWN - 1) * DEPTH + z), BW, 1)
            fourth.append(jnp.where(jnp.logical_and(last, row8 == 0), edge, v))
            after_row = spread(from_next, f, 8 * DEPTH + z)
            before_row = spread(from_prev, f, PREV - DEPTH + z)
            edge = pltpu.roll(spread(raw, f, z), LANES - BW, 1)
            before_row = jnp.where(first, edge, before_row)
            sides.append(jnp.where(row8 == 7, before_row, after_row))
        for i, group in ((OWN // 8, fourth), (OWN // 8 + 1, sides)):
            for f, value in enumerate(conserved(group[:6])):
                ext[f, 2 + z, i * 8 : i * 8 + 8] = value
            ext[6, 2 + z, i * 8 : i * 8 + 8] = 0.5 * group[6]

    plane_copies = [
        halo(3, ext.at[:, pl.ds(4, 2)], low_planes, near_at(1)),
        halo(4, ext.at[:, pl.ds(2, 2)], high_planes, near_at(n_near - 1)),
    ]

    def fill_derived(z):
        for i, value in enumerate(derive([ext[f, z] for f in range(5)])):
            der[i, z] = value

    def cell(z):
        return [ext[f, z] for f in range(6)], [der[i, z] for i in range(6)], ext[6, z]

    def fill_rate(z):
        for f, value in enumerate(plane_rate(cell, z)):
            rate_out[f, z - 1] = value

    lax.fori_loop(2, 6, lambda z, c: (fill_derived(z), c)[1], 0)

    best = gathered(y_copies, got_y, best)
    sent[2] = best
    z_copies = exchange(2, got_z, z_at, n_z, z_send, z_recv)

    lax.fori_loop(3, 5, lambda z, c: (fill_rate(z), c)[1], 0)

    for copy in plane_copies:
        copy.wait()
    for i in range(2):
        for f in range(7):
            ext[f, i] = low_planes[f, i]
            ext[f, 6 + i] = high_planes[f, i]
    for z in (0, 1, 6, 7):
        fill_derived(z)
    lax.fori_loop(0, 2, lambda i, c: (fill_rate(1 + 4 * i), c)[1], 0)
    lax.fori_loop(0, 2, lambda i, c: (fill_rate(2 + 4 * i), c)[1], 0)
    for f in range(7):
        for z in range(6):
            u_out[f, z] = ext[f, z + 1]
    flag_out[0:1] = flag_sent[...]
    flag_out[1:2] = flag_got[...]

    top_out[...] = gathered(z_copies, got_z, best)
    for copy in near_copies + curve_copies + y_copies + z_copies:
        copy.wait_send()


def finish_kernel(n_curve, u_ref, rate_ref, top_ref, flag_ref, out_ref, half, der):
    curve = lax.axis_index("curve")
    first, last = curve == 0, curve == n_curve - 1
    top = top_ref[...]
    lane = lane_of(top.shape)
    speed = jnp.max(jnp.where(lane < LANES // 2, top, 0.0), axis=1, keepdims=True)
    cond = jnp.max(jnp.where(lane < LANES // 2, 0.0, top), axis=1, keepdims=True)
    step = 0.8 / (speed + 6.0 * cond)
    row = row_of((ROWS, LANES))

    def fill_half(z, carry):
        values = []
        for f in range(6):
            v = u_ref[f, z] + step * rate_ref[f, z]
            left = pltpu.roll(jnp.broadcast_to(v[0:1], v.shape), LANES - BW, 1)
            right = pltpu.roll(jnp.broadcast_to(v[OWN - 1 : OWN], v.shape), BW, 1)
            v = jnp.where(jnp.logical_and(first, row == ROWS - 1), left, v)
            v = jnp.where(jnp.logical_and(last, row == OWN), right, v)
            half[f, z] = v
            values.append(v)
        for i, value in enumerate(derive(values[:5])):
            der[i, z] = value
        return carry

    lax.fori_loop(0, 6, fill_half, 0)
    leaving = flag_ref[0:1] > 0.5
    arriving = flag_ref[1:2] > 0.5

    def cell(z):
        return [half[f, z] for f in range(6)], [der[i, z] for i in range(6)], u_ref[6, z]

    def fill_out(z, carry):
        rates = plane_rate(cell, z)
        for f in range(6):
            final = 0.5 * u_ref[f, z] + 0.5 * (half[f, z] + step * rates[f])
            box = [final[8 * j : 8 * j + 8] for j in range(BOXES + 1)]
            slot = [jnp.where(leaving, box[j + 1], box[j]) for j in range(BOXES)]
            slot[2] = jnp.where(jnp.logical_and(leaving, jnp.logical_not(arriving)), 0.0, slot[2])
            slot.append(jnp.where(jnp.logical_and(arriving, jnp.logical_not(leaving)), box[3], 0.0))
            for j, value in enumerate(slot):
                out_ref[f, pl.ds(j * 8 * DEPTH + z - 1, 8, stride=DEPTH)] = value
        return carry

    lax.fori_loop(1, 5, fill_out, 0)


def local(n_curve, n_near, primitive, conductivity, new_owner):
    rows = OWN * DEPTH
    prim = primitive.reshape(6, DEPTH, OWN, LANES).transpose(0, 2, 1, 3).reshape(6, rows, LANES)
    cond = conductivity.reshape(DEPTH, OWN, LANES).transpose(1, 0, 2).reshape(rows, LANES)
    n_y, n_z = Y_CHIPS, n_curve // Y_CHIPS
    anywhere = pl.BlockSpec(memory_space=pl.ANY)
    vmem = pl.BlockSpec(memory_space=pltpu.VMEM)
    dma = pltpu.SemaphoreType.DMA
    state = pl.pallas_call(
        functools.partial(exchange_kernel, n_curve, n_near),
        out_shape=(
            pltpu.VMEM((7, 6, ROWS, LANES), F32),
            pltpu.VMEM((6, 6, ROWS, LANES), F32),
            pltpu.VMEM((1, LANES), F32),
            pltpu.VMEM((2, LANES), F32),
        ),
        in_specs=[anywhere] * 3,
        out_specs=(vmem,) * 4,
        scratch_shapes=[
            pltpu.VMEM((7, rows, LANES), F32),
            pltpu.VMEM((7, NEXT, LANES), F32),
            pltpu.VMEM((7, PREV, LANES), F32),
            pltpu.VMEM((7, 8, ROWS, LANES), F32),
            pltpu.VMEM((6, 8, ROWS, LANES), F32),
            pltpu.VMEM((7, 2, ROWS, LANES), F32),
            pltpu.VMEM((7, 2, ROWS, LANES), F32),
            pltpu.VMEM((3, 1, LANES), F32),
            pltpu.VMEM((n_near - 1, 1, LANES), F32),
            pltpu.VMEM((n_y - 1, 1, LANES), F32),
            pltpu.VMEM((n_z - 1, 1, LANES), F32),
            pltpu.VMEM((1, LANES), F32),
            pltpu.VMEM((1, LANES), F32),
            pltpu.SMEM((BOXES,), jnp.int32),
            dma((3,)),
            dma((n_near - 1,)), dma((n_near - 1,)),
            dma((n_y - 1,)), dma((n_y - 1,)),
            dma((n_z - 1,)), dma((n_z - 1,)),
            dma((5,)), dma((5,)),
        ],
        compiler_params=pltpu.CompilerParams(collective_id=0, has_side_effects=True),
        name="exchange",
    )(prim, cond, new_owner)
    out = pl.pallas_call(
        functools.partial(finish_kernel, n_curve),
        out_shape=jax.ShapeDtypeStruct((6, 32 * DEPTH, LANES), F32),
        in_specs=[vmem] * 4,
        out_specs=vmem,
        scratch_shapes=[pltpu.VMEM((6, 6, ROWS, LANES), F32)] * 2,
        name="finish",
    )(*(pltpu.with_memory_space_constraint(v, pltpu.VMEM) for v in state))
    out = out.reshape(6, 32, DEPTH, LANES).transpose(0, 2, 1, 3).reshape(6, DEPTH, 32 * LANES)
    return out[None]


def solution(mesh):
    n_curve, n_near = mesh.shape["curve"], mesh.shape["near"]
    return jax.shard_map(
        functools.partial(local, n_curve, n_near),
        mesh=mesh,
        in_specs=(P(None, "near", "curve"), P("near", "curve"), P("curve")),
        out_specs=P("curve", None, "near", None),
        check_vma=False,
    )
```

```python
import functools

import jax
import jax.numpy as jnp
from jax import lax
from jax.experimental import pallas as pl
from jax.experimental.pallas import tpu as pltpu
from jax.sharding import PartitionSpec as P

BW = 32
BOXES = 3
DEPTH = 4
LANES = 128
OWN = 24
ROWS = 40
NEXT = 40
PREV = 8
Y_CHIPS = 8
RELAY = 3
MESH = pl.DeviceIdType.MESH
F32 = jnp.float32


def lane_of(shape):
    return lax.broadcasted_iota(jnp.int32, shape, len(shape) - 1)


def row_of(shape):
    return lax.broadcasted_iota(jnp.int32, shape, 0)


def upper_y(v, ypos):
    return jnp.where(ypos == BW - 1, pltpu.roll(v, BW - 1, 1), pltpu.roll(v, LANES - 1, 1))


def lower_y(v, ypos):
    return jnp.where(ypos == 0, pltpu.roll(v, LANES - BW + 1, 1), pltpu.roll(v, 1, 1))


def upper_x(v, lane):
    above = pltpu.roll(v, v.shape[0] - 1, 0)
    return pltpu.roll(jnp.where(lane < BW, above, v), LANES - BW, 1)


def lower_x(v, lane):
    below = pltpu.roll(v, 1, 0)
    return pltpu.roll(jnp.where(lane >= LANES - BW, below, v), BW, 1)


def derive(cons):
    r, mx, my, mz, energy = cons[:5]
    inv = 1.0 / r
    vx, vy, vz = mx * inv, my * inv, mz * inv
    pressure = 0.4 * (energy - 0.5 * (mx * vx + my * vy + mz * vz))
    temp = pressure * inv
    return 0.5 * vx, 0.5 * vy, 0.5 * vz, 0.5 * jnp.sqrt(1.4 * temp), 0.5 * pressure, temp


def face(lo, hi, k):
    lu, ld, lc = lo
    hu, hd, hc = hi
    lw, hw = ld[k], hd[k]
    top = jnp.maximum(jnp.abs(lw) + ld[3], jnp.abs(hw) + hd[3])
    lf, hf = lw + top, hw - top
    flux = [a * lf + b * hf for a, b in zip(lu, hu)]
    flux[1 + k] = flux[1 + k] + (ld[4] + hd[4])
    work = ld[4] * lw + hd[4] * hw
    flux[4] = flux[4] + (work + work) - (lc + hc) * (hd[5] - ld[5])
    return flux


def mapped(cell, fn):
    u, d, c = cell
    return [fn(a) for a in u], [fn(a) for a in d], fn(c)


def plane_rate(get, z):
    mid = get(z)
    shape = mid[2].shape
    lane = lane_of(shape)
    ypos = lane % BW
    flux = face(mid, mapped(mid, lambda v: upper_x(v, lane)), 0)
    total = [lower_x(f, lane) - f for f in flux]
    flux = face(mid, mapped(mid, lambda v: upper_y(v, ypos)), 1)
    total = [t + (lower_y(f, ypos) - f) for t, f in zip(total, flux)]
    flux = face(mid, get(z + 1), 2)
    total = [t - f for t, f in zip(total, flux)]
    flux = face(get(z - 1), mid, 2)
    return [t + f for t, f in zip(total, flux)]


def spread(ref, f, row):
    return jnp.broadcast_to(ref[f, row : row + 1], (8, LANES))


def conserved(prim):
    r, vx, vy, vz, p, s = prim
    energy = p * 2.5 + 0.5 * r * (vx * vx + vy * vy + vz * vz)
    return r, r * vx, r * vy, r * vz, energy, r * s


def exchange_kernel(
    n_curve, n_near,
    prim_hbm, cond_hbm, owner_hbm,
    u_out, rate_out, top_out, flag_out,
    raw, from_next, from_prev, ext, der, low_planes, high_planes,
    sent, got_plane, got_column, flag_sent, flag_got, owner,
    load_sem, stage_send, stage_recv, halo_send, halo_recv, relay,
):
    n_y, n_x = Y_CHIPS, n_near // 2
    n_z = n_curve // n_y
    curve, near = lax.axis_index("curve"), lax.axis_index("near")
    y, z_chip, x, core = lax.rem(curve, n_y), lax.div(curve, n_y), lax.div(near, 2), lax.rem(near, 2)
    first, last = curve == 0, curve == n_curve - 1
    loads = [
        pltpu.make_async_copy(prim_hbm, raw.at[pl.ds(0, 6)], load_sem.at[0]),
        pltpu.make_async_copy(cond_hbm, raw.at[6], load_sem.at[1]),
        pltpu.make_async_copy(owner_hbm, owner, load_sem.at[2]),
    ]
    for copy in loads:
        copy.start()

    def ring(j, n):
        return min(j % n, -j % n)

    ys = [lax.rem(y + j, n_y) for j in range(n_y)]
    xs = [2 * lax.rem(x + j, n_x) for j in range(n_x)]
    zs = [n_y * lax.rem(z_chip + j, n_z) for j in range(n_z)]

    def plane_at(offset, side):
        return (zs[0] + ys[offset[1]], xs[offset[0]] + side)

    def column_at(j, side):
        return (zs[j] + ys[0], xs[0] + side)

    plane = sorted(
        ((i, j) for i in range(n_x) for j in range(n_y)),
        key=lambda o: -ring(o[0], n_x) - ring(o[1], n_y),
    )
    slot_of = {o: o[0] * n_y + o[1] for o in plane}
    others = [o for o in plane if slot_of[o] > 0]
    n_plane = len(plane)
    column = sorted(range(n_z), key=lambda j: -ring(j, n_z))
    close = [j for j in column if 0 < ring(j, n_z) <= RELAY]
    relays = [RELAY, n_z - RELAY] if n_z // 2 > RELAY else []
    before, after = (lax.rem(curve + n_curve - 1, n_curve), near), (lax.rem(curve + 1, n_curve), near)
    barrier = pltpu.get_barrier_semaphore()

    def greet(devices):
        for device in devices:
            pl.semaphore_signal(barrier, inc=1, device_id=device, device_id_type=MESH)

    @pl.when(core == 0)
    def _():
        greet([plane_at(o, 1) for o in plane] + [column_at(j, 1) for j in close])

    @pl.when(core == 1)
    def _():
        greet([plane_at(o, 1) for o in others] + [plane_at(o, 0) for o in plane])
        greet([column_at(j, 1) for j in close])

    greet([before, after])

    for copy in loads:
        copy.wait()
    speed, cond = None, None
    for i in range(0, raw.shape[1], 8):
        r, vx, vy, vz, p = (raw[f, i : i + 8] for f in range(5))
        here = jnp.abs(vx) + jnp.abs(vy) + jnp.abs(vz) + 3.0 * jnp.sqrt(1.4 * p / r)
        k = raw[6, i : i + 8]
        speed = here if speed is None else jnp.maximum(speed, here)
        cond = k if cond is None else jnp.maximum(cond, k)
    lane8 = lane_of((8, LANES))
    both = jnp.where(
        lane8 < LANES // 2,
        jnp.maximum(speed, pltpu.roll(speed, LANES // 2, 1)),
        jnp.maximum(cond, pltpu.roll(cond, LANES // 2, 1)),
    )
    best = jnp.max(both, axis=0, keepdims=True)
    sent[0] = best
    leaving = jnp.where(owner[0] != curve, 1.0, 0.0).astype(F32)
    flag_sent[...] = jnp.full(flag_sent.shape, leaving, F32)

    def send(stage, got, slot, device):
        pltpu.make_async_remote_copy(
            src_ref=sent.at[stage], dst_ref=got.at[slot], send_sem=stage_send.at[stage],
            recv_sem=stage_recv.at[stage], device_id=device, device_id_type=MESH,
        ).start()

    def wait_rows(sem, got, count):
        rows = got.at[pl.ds(0, count)]
        pltpu.make_async_copy(rows, rows, sem).wait()

    def largest(rows):
        while len(rows) > 1:
            rows = [jnp.maximum(*rows[i : i + 2]) if i + 1 < len(rows) else rows[i] for i in range(0, len(rows), 2)]
        return rows[0]

    def halo(i, src, dst, device):
        return pltpu.make_async_remote_copy(
            src_ref=src, dst_ref=dst, send_sem=halo_send.at[i], recv_sem=halo_recv.at[i],
            device_id=device, device_id_type=MESH,
        )

    @pl.when(core == 0)
    def _():
        pl.semaphore_wait(barrier, n_plane + 2)
        for o in plane:
            send(0, got_plane, n_plane - 1 + slot_of[o], plane_at(o, 1))

    @pl.when(core == 1)
    def _():
        pl.semaphore_wait(barrier, 2 * n_plane - 1 + 2 * len(close) + 2)
        for j in relays:
            pl.semaphore_signal(relay, inc=1, device_id=column_at(j, 1), device_id_type=MESH)
        for o in others:
            send(0, got_plane, slot_of[o] - 1, plane_at(o, 1))

    to_before = [halo(0, raw.at[:, pl.ds(0, NEXT)], from_next, before), halo(2, flag_sent, flag_got, before)]
    to_after = [halo(1, raw.at[:, pl.ds(raw.shape[1] - PREV, PREV)], from_prev, after)]

    @pl.when(jnp.logical_not(first))
    def _():
        for copy in to_before:
            copy.start()

    @pl.when(jnp.logical_not(last))
    def _():
        for copy in to_after:
            copy.start()

    for z in range(DEPTH):
        for i in range(OWN // 8):
            rows = pl.ds(i * 8 * DEPTH + z, 8, stride=DEPTH)
            for f, value in enumerate(conserved([raw[f, rows] for f in range(6)])):
                ext[f, 2 + z, i * 8 : i * 8 + 8] = value
            ext[6, 2 + z, i * 8 : i * 8 + 8] = 0.5 * raw[6, rows]

    @pl.when(core == 1)
    def _():
        count = 2 * n_plane - 1
        wait_rows(stage_recv.at[0], got_plane, count)
        sent[1] = largest([sent[0]] + [got_plane[i] for i in range(count)])
        if relays:
            pl.semaphore_wait(relay, len(relays))
        for j in column:
            send(1, got_column, j, column_at(j, 0))
            if j:
                send(1, got_column, j - 1, column_at(j, 1))

    row8 = row_of((8, LANES))

    @pl.when(jnp.logical_not(last))
    def _():
        for copy in to_before:
            copy.wait_recv()

    @pl.when(jnp.logical_not(first))
    def _():
        for copy in to_after:
            copy.wait_recv()

    for z in range(DEPTH):
        fourth, sides = [], []
        for f in range(7):
            v = from_next[f, pl.ds(z, 8, stride=DEPTH)]
            edge = pltpu.roll(spread(raw, f, (OWN - 1) * DEPTH + z), BW, 1)
            fourth.append(jnp.where(jnp.logical_and(last, row8 == 0), edge, v))
            after_row = spread(from_next, f, 8 * DEPTH + z)
            before_row = spread(from_prev, f, PREV - DEPTH + z)
            edge = pltpu.roll(spread(raw, f, z), LANES - BW, 1)
            before_row = jnp.where(first, edge, before_row)
            sides.append(jnp.where(row8 == 7, before_row, after_row))
        for i, group in ((OWN // 8, fourth), (OWN // 8 + 1, sides)):
            for f, value in enumerate(conserved(group[:6])):
                ext[f, 2 + z, i * 8 : i * 8 + 8] = value
            ext[6, 2 + z, i * 8 : i * 8 + 8] = 0.5 * group[6]

    plane_copies = [
        halo(3, ext.at[:, pl.ds(4, 2)], low_planes, (curve, lax.rem(near + 1, n_near))),
        halo(4, ext.at[:, pl.ds(2, 2)], high_planes, (curve, lax.rem(near + n_near - 1, n_near))),
    ]
    for copy in plane_copies:
        copy.start()

    def fill_derived(z):
        for i, value in enumerate(derive([ext[f, z] for f in range(5)])):
            der[i, z] = value

    def cell(z):
        return [ext[f, z] for f in range(6)], [der[i, z] for i in range(6)], ext[6, z]

    def fill_rate(z):
        for f, value in enumerate(plane_rate(cell, z)):
            rate_out[f, z - 1] = value

    lax.fori_loop(2, 6, lambda z, c: (fill_derived(z), c)[1], 0)

    lax.fori_loop(3, 5, lambda z, c: (fill_rate(z), c)[1], 0)

    for copy in plane_copies:
        copy.wait()
    for i in range(2):
        for f in range(7):
            ext[f, i] = low_planes[f, i]
            ext[f, 6 + i] = high_planes[f, i]
    for z in (0, 1, 6, 7):
        fill_derived(z)
    lax.fori_loop(0, 2, lambda i, c: (fill_rate(1 + 4 * i), c)[1], 0)
    lax.fori_loop(0, 2, lambda i, c: (fill_rate(2 + 4 * i), c)[1], 0)
    for f in range(7):
        for z in range(6):
            u_out[f, z] = ext[f, z + 1]
    flag_out[0:1] = flag_sent[...]
    flag_out[1:2] = jnp.where(last, 0.0, flag_got[...])

    @pl.when(jnp.logical_not(first))
    def _():
        for copy in to_before:
            copy.wait_send()

    @pl.when(jnp.logical_not(last))
    def _():
        for copy in to_after:
            copy.wait_send()

    @pl.when(core == 0)
    def _():
        wait_rows(stage_send.at[0], got_plane, n_plane)
        wait_rows(stage_recv.at[1], got_column, n_z)
        top_out[...] = largest([got_column[i] for i in range(n_z)])

    @pl.when(core == 1)
    def _():
        wait_rows(stage_send.at[0], got_plane, n_plane - 1)
        wait_rows(stage_recv.at[1], got_column, n_z - 1)
        top_out[...] = largest([sent[1]] + [got_column[i] for i in range(n_z - 1)])
        wait_rows(stage_send.at[1], got_plane, 2 * n_z - 1)


def finish_kernel(n_curve, u_ref, rate_ref, top_ref, flag_ref, out_ref, half, der):
    curve = lax.axis_index("curve")
    first, last = curve == 0, curve == n_curve - 1
    top = top_ref[...]
    lane = lane_of(top.shape)
    speed = jnp.max(jnp.where(lane < LANES // 2, top, 0.0), axis=1, keepdims=True)
    cond = jnp.max(jnp.where(lane < LANES // 2, 0.0, top), axis=1, keepdims=True)
    step = 0.8 / (speed + 6.0 * cond)
    row = row_of((ROWS, LANES))

    def fill_half(z, carry):
        values = []
        for f in range(6):
            v = u_ref[f, z] + step * rate_ref[f, z]
            left = pltpu.roll(jnp.broadcast_to(v[0:1], v.shape), LANES - BW, 1)
            right = pltpu.roll(jnp.broadcast_to(v[OWN - 1 : OWN], v.shape), BW, 1)
            v = jnp.where(jnp.logical_and(first, row == ROWS - 1), left, v)
            v = jnp.where(jnp.logical_and(last, row == OWN), right, v)
            half[f, z] = v
            values.append(v)
        for i, value in enumerate(derive(values[:5])):
            der[i, z] = value
        return carry

    lax.fori_loop(0, 6, fill_half, 0)
    leaving = flag_ref[0:1] > 0.5
    arriving = flag_ref[1:2] > 0.5

    def cell(z):
        return [half[f, z] for f in range(6)], [der[i, z] for i in range(6)], u_ref[6, z]

    def fill_out(z, carry):
        rates = plane_rate(cell, z)
        for f in range(6):
            final = 0.5 * u_ref[f, z] + 0.5 * (half[f, z] + step * rates[f])
            box = [final[8 * j : 8 * j + 8] for j in range(BOXES + 1)]
            slot = [jnp.where(leaving, box[j + 1], box[j]) for j in range(BOXES)]
            slot[2] = jnp.where(jnp.logical_and(leaving, jnp.logical_not(arriving)), 0.0, slot[2])
            slot.append(jnp.where(jnp.logical_and(arriving, jnp.logical_not(leaving)), box[3], 0.0))
            for j, value in enumerate(slot):
                out_ref[f, pl.ds(j * 8 * DEPTH + z - 1, 8, stride=DEPTH)] = value
        return carry

    lax.fori_loop(1, 5, fill_out, 0)


def local(n_curve, n_near, primitive, conductivity, new_owner):
    rows = OWN * DEPTH
    prim = primitive.reshape(6, DEPTH, OWN, LANES).transpose(0, 2, 1, 3).reshape(6, rows, LANES)
    cond = conductivity.reshape(DEPTH, OWN, LANES).transpose(1, 0, 2).reshape(rows, LANES)
    n_y, n_z = Y_CHIPS, n_curve // Y_CHIPS
    anywhere = pl.BlockSpec(memory_space=pl.ANY)
    vmem = pl.BlockSpec(memory_space=pltpu.VMEM)
    dma = pltpu.SemaphoreType.DMA
    state = pl.pallas_call(
        functools.partial(exchange_kernel, n_curve, n_near),
        out_shape=(
            pltpu.VMEM((7, 6, ROWS, LANES), F32),
            pltpu.VMEM((6, 6, ROWS, LANES), F32),
            pltpu.VMEM((1, LANES), F32),
            pltpu.VMEM((2, LANES), F32),
        ),
        in_specs=[anywhere] * 3,
        out_specs=(vmem,) * 4,
        scratch_shapes=[
            pltpu.VMEM((7, rows, LANES), F32),
            pltpu.VMEM((7, NEXT, LANES), F32),
            pltpu.VMEM((7, PREV, LANES), F32),
            pltpu.VMEM((7, 8, ROWS, LANES), F32),
            pltpu.VMEM((6, 8, ROWS, LANES), F32),
            pltpu.VMEM((7, 2, ROWS, LANES), F32),
            pltpu.VMEM((7, 2, ROWS, LANES), F32),
            pltpu.VMEM((2, 1, LANES), F32),
            pltpu.VMEM((max(n_near * n_y - 1, 2 * n_z - 1), 1, LANES), F32),
            pltpu.VMEM((n_z, 1, LANES), F32),
            pltpu.VMEM((1, LANES), F32),
            pltpu.VMEM((1, LANES), F32),
            pltpu.SMEM((BOXES,), jnp.int32),
            dma((3,)),
            dma((2,)),
            dma((2,)),
            dma((5,)),
            dma((5,)),
            pltpu.SemaphoreType.REGULAR,
        ],
        compiler_params=pltpu.CompilerParams(collective_id=0, has_side_effects=True),
        name="exchange",
    )(prim, cond, new_owner)
    out = pl.pallas_call(
        functools.partial(finish_kernel, n_curve),
        out_shape=jax.ShapeDtypeStruct((6, 32 * DEPTH, LANES), F32),
        in_specs=[vmem] * 4,
        out_specs=vmem,
        scratch_shapes=[pltpu.VMEM((6, 6, ROWS, LANES), F32)] * 2,
        name="finish",
    )(*(pltpu.with_memory_space_constraint(v, pltpu.VMEM) for v in state))
    out = out.reshape(6, 32, DEPTH, LANES).transpose(0, 2, 1, 3).reshape(6, DEPTH, 32 * LANES)
    return out[None]


def solution(mesh):
    n_curve, n_near = mesh.shape["curve"], mesh.shape["near"]
    return jax.shard_map(
        functools.partial(local, n_curve, n_near),
        mesh=mesh,
        in_specs=(P(None, "near", "curve"), P("near", "curve"), P("curve")),
        out_specs=P("curve", None, "near", None),
        check_vma=False,
    )
```

```python
import functools

import jax
import jax.numpy as jnp
from jax import lax
from jax.experimental import pallas as pl
from jax.experimental.pallas import tpu as pltpu
from jax.sharding import PartitionSpec as P

BW = 32
BOXES = 3
DEPTH = 4
LANES = 128
OWN = 24
ROWS = 40
NEXT = 40
PREV = 8
Y_CHIPS = 8
VMEM_LIMIT = 48 << 20
RELAY = 3
MESH = pl.DeviceIdType.MESH
F32 = jnp.float32


def lane_of(shape):
    return lax.broadcasted_iota(jnp.int32, shape, len(shape) - 1)


def row_of(shape):
    return lax.broadcasted_iota(jnp.int32, shape, 0)


def upper_y(v, ypos):
    return jnp.where(ypos == BW - 1, pltpu.roll(v, BW - 1, 1), pltpu.roll(v, LANES - 1, 1))


def lower_y(v, ypos):
    return jnp.where(ypos == 0, pltpu.roll(v, LANES - BW + 1, 1), pltpu.roll(v, 1, 1))


def upper_x(v, lane):
    above = pltpu.roll(v, v.shape[0] - 1, 0)
    return pltpu.roll(jnp.where(lane < BW, above, v), LANES - BW, 1)


def lower_x(v, lane):
    below = pltpu.roll(v, 1, 0)
    return pltpu.roll(jnp.where(lane >= LANES - BW, below, v), BW, 1)


def derive(cons):
    r, mx, my, mz, energy = cons[:5]
    inv = 1.0 / r
    vx, vy, vz = mx * inv, my * inv, mz * inv
    pressure = 0.4 * (energy - 0.5 * (mx * vx + my * vy + mz * vz))
    temp = pressure * inv
    return 0.5 * vx, 0.5 * vy, 0.5 * vz, 0.5 * jnp.sqrt(1.4 * temp), 0.5 * pressure, temp


def face(lo, hi, k):
    lu, ld, lc = lo
    hu, hd, hc = hi
    lw, hw = ld[k], hd[k]
    top = jnp.maximum(jnp.abs(lw) + ld[3], jnp.abs(hw) + hd[3])
    lf, hf = lw + top, hw - top
    flux = [a * lf + b * hf for a, b in zip(lu, hu)]
    flux[1 + k] = flux[1 + k] + (ld[4] + hd[4])
    work = ld[4] * lw + hd[4] * hw
    flux[4] = flux[4] + (work + work) - (lc + hc) * (hd[5] - ld[5])
    return flux


def mapped(cell, fn):
    u, d, c = cell
    return [fn(a) for a in u], [fn(a) for a in d], fn(c)


def plane_rate(get, z):
    mid = get(z)
    shape = mid[2].shape
    lane = lane_of(shape)
    ypos = lane % BW
    flux = face(mid, mapped(mid, lambda v: upper_x(v, lane)), 0)
    total = [lower_x(f, lane) - f for f in flux]
    flux = face(mid, mapped(mid, lambda v: upper_y(v, ypos)), 1)
    total = [t + (lower_y(f, ypos) - f) for t, f in zip(total, flux)]
    flux = face(mid, get(z + 1), 2)
    total = [t - f for t, f in zip(total, flux)]
    flux = face(get(z - 1), mid, 2)
    return [t + f for t, f in zip(total, flux)]


def spread(ref, f, row):
    return jnp.broadcast_to(ref[f, row : row + 1], (8, LANES))


def conserved(prim):
    r, vx, vy, vz, p, s = prim
    energy = p * 2.5 + 0.5 * r * (vx * vx + vy * vy + vz * vz)
    return r, r * vx, r * vy, r * vz, energy, r * s


def exchange_kernel(
    n_curve, n_near,
    prim_hbm, cond_hbm, owner_hbm,
    u_out, rate_out, u_side, rate_side, top_out, flag_out,
    raw, from_next, from_prev, ext, der, low_planes, high_planes,
    sent, got_plane, got_column, flag_sent, flag_got, owner,
    load_sem, stage_send, stage_recv, halo_send, halo_recv, relay,
):
    n_y, n_x = Y_CHIPS, n_near // 2
    n_z = n_curve // n_y
    curve, near = lax.axis_index("curve"), lax.axis_index("near")
    y, z_chip, x, core = lax.rem(curve, n_y), lax.div(curve, n_y), lax.div(near, 2), lax.rem(near, 2)
    first, last = curve == 0, curve == n_curve - 1
    loads = [
        pltpu.make_async_copy(prim_hbm, raw.at[pl.ds(0, 6)], load_sem.at[0]),
        pltpu.make_async_copy(cond_hbm, raw.at[6], load_sem.at[1]),
        pltpu.make_async_copy(owner_hbm, owner, load_sem.at[2]),
    ]
    for copy in loads:
        copy.start()

    def ring(j, n):
        return min(j % n, -j % n)

    ys = [lax.rem(y + j, n_y) for j in range(n_y)]
    xs = [2 * lax.rem(x + j, n_x) for j in range(n_x)]
    zs = [n_y * lax.rem(z_chip + j, n_z) for j in range(n_z)]

    def plane_at(offset, side):
        return (zs[0] + ys[offset[1]], xs[offset[0]] + side)

    def column_at(j, side):
        return (zs[j] + ys[0], xs[0] + side)

    plane = sorted(
        ((i, j) for i in range(n_x) for j in range(n_y)),
        key=lambda o: -ring(o[0], n_x) - ring(o[1], n_y),
    )
    slot_of = {o: o[0] * n_y + o[1] for o in plane}
    others = [o for o in plane if slot_of[o] > 0]
    n_plane = len(plane)
    column = sorted(range(n_z), key=lambda j: -ring(j, n_z))
    close = [j for j in column if 0 < ring(j, n_z) <= RELAY]
    relays = [RELAY, n_z - RELAY] if n_z // 2 > RELAY else []
    before, after = (lax.rem(curve + n_curve - 1, n_curve), near), (lax.rem(curve + 1, n_curve), near)
    barrier = pltpu.get_barrier_semaphore()

    def greet(devices):
        for device in devices:
            pl.semaphore_signal(barrier, inc=1, device_id=device, device_id_type=MESH)

    @pl.when(core == 0)
    def _():
        greet([plane_at(o, 1) for o in plane] + [column_at(j, 1) for j in close])

    @pl.when(core == 1)
    def _():
        greet([plane_at(o, 1) for o in others] + [plane_at(o, 0) for o in plane])
        greet([column_at(j, 1) for j in close])

    greet([before, after])

    for copy in loads:
        copy.wait()
    speed, cond = None, None
    for i in range(0, raw.shape[1], 8):
        r, vx, vy, vz, p = (raw[f, i : i + 8] for f in range(5))
        here = jnp.abs(vx) + jnp.abs(vy) + jnp.abs(vz) + 3.0 * jnp.sqrt(1.4 * p / r)
        k = raw[6, i : i + 8]
        speed = here if speed is None else jnp.maximum(speed, here)
        cond = k if cond is None else jnp.maximum(cond, k)
    lane8 = lane_of((8, LANES))
    both = jnp.where(
        lane8 < LANES // 2,
        jnp.maximum(speed, pltpu.roll(speed, LANES // 2, 1)),
        jnp.maximum(cond, pltpu.roll(cond, LANES // 2, 1)),
    )
    best = jnp.max(both, axis=0, keepdims=True)
    sent[0] = best
    leaving = jnp.where(owner[0] != curve, 1.0, 0.0).astype(F32)
    flag_sent[...] = jnp.full(flag_sent.shape, leaving, F32)

    def send(stage, got, slot, device):
        pltpu.make_async_remote_copy(
            src_ref=sent.at[stage], dst_ref=got.at[slot], send_sem=stage_send.at[stage],
            recv_sem=stage_recv.at[stage], device_id=device, device_id_type=MESH,
        ).start()

    def wait_rows(sem, got, count):
        rows = got.at[pl.ds(0, count)]
        pltpu.make_async_copy(rows, rows, sem).wait()

    def largest(rows):
        while len(rows) > 1:
            rows = [jnp.maximum(*rows[i : i + 2]) if i + 1 < len(rows) else rows[i] for i in range(0, len(rows), 2)]
        return rows[0]

    def halo(i, src, dst, device):
        return pltpu.make_async_remote_copy(
            src_ref=src, dst_ref=dst, send_sem=halo_send.at[i], recv_sem=halo_recv.at[i],
            device_id=device, device_id_type=MESH,
        )

    @pl.when(core == 0)
    def _():
        pl.semaphore_wait(barrier, n_plane + 2)
        for o in plane:
            send(0, got_plane, n_plane - 1 + slot_of[o], plane_at(o, 1))

    @pl.when(core == 1)
    def _():
        pl.semaphore_wait(barrier, 2 * n_plane - 1 + 2 * len(close) + 2)
        for j in relays:
            pl.semaphore_signal(relay, inc=1, device_id=column_at(j, 1), device_id_type=MESH)
        for o in others:
            send(0, got_plane, slot_of[o] - 1, plane_at(o, 1))

    to_before = [halo(0, raw.at[:, pl.ds(0, NEXT)], from_next, before), halo(2, flag_sent, flag_got, before)]
    to_after = [halo(1, raw.at[:, pl.ds(raw.shape[1] - PREV, PREV)], from_prev, after)]

    @pl.when(jnp.logical_not(first))
    def _():
        for copy in to_before:
            copy.start()

    @pl.when(jnp.logical_not(last))
    def _():
        for copy in to_after:
            copy.start()

    for z in range(DEPTH):
        for i in range(OWN // 8):
            rows = pl.ds(i * 8 * DEPTH + z, 8, stride=DEPTH)
            for f, value in enumerate(conserved([raw[f, rows] for f in range(6)])):
                ext[f, 2 + z, i * 8 : i * 8 + 8] = value
            ext[6, 2 + z, i * 8 : i * 8 + 8] = 0.5 * raw[6, rows]

    @pl.when(core == 1)
    def _():
        count = 2 * n_plane - 1
        wait_rows(stage_recv.at[0], got_plane, count)
        sent[1] = largest([sent[0]] + [got_plane[i] for i in range(count)])
        if relays:
            pl.semaphore_wait(relay, len(relays))
        for j in column:
            send(1, got_column, j, column_at(j, 0))
            if j:
                send(1, got_column, j - 1, column_at(j, 1))

    row8 = row_of((8, LANES))

    @pl.when(jnp.logical_not(last))
    def _():
        for copy in to_before:
            copy.wait_recv()

    @pl.when(jnp.logical_not(first))
    def _():
        for copy in to_after:
            copy.wait_recv()

    for z in range(DEPTH):
        fourth, sides = [], []
        for f in range(7):
            v = from_next[f, pl.ds(z, 8, stride=DEPTH)]
            edge = pltpu.roll(spread(raw, f, (OWN - 1) * DEPTH + z), BW, 1)
            fourth.append(jnp.where(jnp.logical_and(last, row8 == 0), edge, v))
            after_row = spread(from_next, f, 8 * DEPTH + z)
            before_row = spread(from_prev, f, PREV - DEPTH + z)
            edge = pltpu.roll(spread(raw, f, z), LANES - BW, 1)
            before_row = jnp.where(first, edge, before_row)
            sides.append(jnp.where(row8 == 7, before_row, after_row))
        for i, group in ((OWN // 8, fourth), (OWN // 8 + 1, sides)):
            for f, value in enumerate(conserved(group[:6])):
                ext[f, 2 + z, i * 8 : i * 8 + 8] = value
            ext[6, 2 + z, i * 8 : i * 8 + 8] = 0.5 * group[6]

    plane_copies = [
        halo(3, ext.at[:, pl.ds(4, 2)], low_planes, (curve, lax.rem(near + 1, n_near))),
        halo(4, ext.at[:, pl.ds(2, 2)], high_planes, (curve, lax.rem(near + n_near - 1, n_near))),
    ]
    for copy in plane_copies:
        copy.start()

    def fill_derived(z):
        for i, value in enumerate(derive([ext[f, z] for f in range(5)])):
            der[i, z] = value

    def cell(z):
        return [ext[f, z] for f in range(6)], [der[i, z] for i in range(6)], ext[6, z]

    row = row_of((ROWS, LANES))
    left_edge = jnp.logical_and(first, row == ROWS - 1)
    right_edge = jnp.logical_and(last, row == OWN)

    def fill_rate(z):
        for f, value in enumerate(plane_rate(cell, z)):
            left = pltpu.roll(jnp.broadcast_to(value[0:1], value.shape), LANES - BW, 1)
            right = pltpu.roll(jnp.broadcast_to(value[OWN - 1 : OWN], value.shape), BW, 1)
            rate_out[f, z - 1] = jnp.where(right_edge, right, jnp.where(left_edge, left, value))

    def fill_sides(z):
        lane = lane_of((ROWS, LANES))
        for f in range(7):
            for ref, of in ((u_side, ext[f, z + 2]),) + (((rate_side, rate_out[f, z + 1]),) if f < 6 else ()):
                ref[0, f, z] = upper_x(of, lane)
                ref[1, f, z] = upper_y(of, lane % BW)

    lax.fori_loop(2, 6, lambda z, c: (fill_derived(z), c)[1], 0)

    lax.fori_loop(3, 5, lambda z, c: (fill_rate(z), c)[1], 0)

    for copy in plane_copies:
        copy.wait()
    for i in range(2):
        for f in range(7):
            ext[f, i] = low_planes[f, i]
            ext[f, 6 + i] = high_planes[f, i]
    for z in (0, 1, 6, 7):
        fill_derived(z)
    lax.fori_loop(0, 2, lambda i, c: (fill_rate(1 + 4 * i), c)[1], 0)
    lax.fori_loop(0, 2, lambda i, c: (fill_rate(2 + 4 * i), c)[1], 0)
    lax.fori_loop(0, DEPTH, lambda z, c: (fill_sides(z), c)[1], 0)
    for f in range(7):
        for z in range(6):
            u_out[f, z] = ext[f, z + 1]
    flag_out[0:1] = flag_sent[...]
    flag_out[1:2] = jnp.where(last, 0.0, flag_got[...])

    @pl.when(jnp.logical_not(first))
    def _():
        for copy in to_before:
            copy.wait_send()

    @pl.when(jnp.logical_not(last))
    def _():
        for copy in to_after:
            copy.wait_send()

    @pl.when(core == 0)
    def _():
        wait_rows(stage_send.at[0], got_plane, n_plane)
        wait_rows(stage_recv.at[1], got_column, n_z)
        top_out[...] = largest([got_column[i] for i in range(n_z)])

    @pl.when(core == 1)
    def _():
        wait_rows(stage_send.at[0], got_plane, n_plane - 1)
        wait_rows(stage_recv.at[1], got_column, n_z - 1)
        top_out[...] = largest([sent[1]] + [got_column[i] for i in range(n_z - 1)])
        wait_rows(stage_send.at[1], got_plane, 2 * n_z - 1)


def beside_y(v, by):
    lane = lane_of(v.shape)
    wanted = lane - lane % BW + (lane + by) % BW
    return jnp.take_along_axis(v, wanted, axis=1, mode="promise_in_bounds")


def with_pressure(u, w, c, k):
    temp = c * c
    return u, w, c, k, temp, u[0] * (temp * (0.5 / 0.35))


def second_face(lo, hi, k):
    (lu, lw, lc, lk, lt, lp), (hu, hw, hc, hk, ht, hp) = lo, hi
    top = jnp.maximum(jnp.abs(lw) + lc, jnp.abs(hw) + hc)
    lf, hf = lw + top, hw - top
    flux = [a * lf + b * hf for a, b in zip(lu, hu)]
    flux[1 + k] = flux[1 + k] + (lp + hp)
    work = lp * lw + hp * hw
    flux[4] = flux[4] + (work + work) - ((lk + hk) * (1.0 / 0.35)) * (ht - lt)
    return flux


def finish_kernel(u_ref, rate_ref, u_side, rate_side, top_ref, flag_ref, out_ref, half, der, low_faces):
    top = top_ref[...]
    lane = lane_of(top.shape)
    speed = jnp.max(jnp.where(lane < LANES // 2, top, 0.0), axis=1, keepdims=True)
    cond = jnp.max(jnp.where(lane < LANES // 2, 0.0, top), axis=1, keepdims=True)
    step = jnp.broadcast_to(0.8 / (speed + 6.0 * cond), (8, LANES))
    chunks = ROWS // 8
    lane, row = lane_of((8, LANES)), row_of((8, LANES))

    def fill_half(z, carry):
        for i in range(chunks):
            rows = pl.ds(8 * i, 8)
            values = [u_ref[f, z, rows] + step * rate_ref[f, z, rows] for f in range(6)]
            for f in range(6):
                half[f, z, rows] = values[f]
            for k, value in enumerate(derive(values[:5])[:4]):
                der[k, z, rows] = value
        return carry

    lax.fori_loop(0, 6, fill_half, 0)
    leaving = flag_ref[0:1] > 0.5
    arriving = flag_ref[1:2] > 0.5
    emptied = jnp.logical_and(leaving, jnp.logical_not(arriving))
    filled = jnp.logical_and(arriving, jnp.logical_not(leaving))
    half_step = 0.5 * step

    def fields(z, i):
        return [half[f, z, pl.ds(8 * i, 8)] for f in range(6)]

    def chunk(z, i, k, u):
        rows = pl.ds(8 * i, 8)
        return with_pressure(u, der[k, z, rows], der[3, z, rows], u_ref[6, z, rows])

    def side(k, z, i, w, c):
        rows = pl.ds(8 * i, 8)
        u = [u_side[k, f, z - 1, rows] + step * rate_side[k, f, z - 1, rows] for f in range(6)]
        return with_pressure(u, w, c, u_side[k, 6, z - 1, rows])

    def x_faces(z, i, u):
        def beside(k):
            if i == chunks - 1:
                above = jnp.broadcast_to(der[k, z, 0:1], (8, LANES))
            else:
                above = der[k, z, pl.ds(8 * i + 1, 8)]
            return pltpu.roll(jnp.where(lane < BW, above, der[k, z, pl.ds(8 * i, 8)]), LANES - BW, 1)

        return second_face(chunk(z, i, 0, u), side(0, z, i, beside(0), beside(3)), 0)

    def y_faces(z, i, u):
        rows = pl.ds(8 * i, 8)
        w, c = beside_y(der[1, z, rows], 1), beside_y(der[3, z, rows], 1)
        return second_face(chunk(z, i, 1, u), side(1, z, i, w, c), 1)

    def z_faces(z, i, u):
        return second_face(chunk(z, i, 2, u), chunk(z + 1, i, 2, fields(z + 1, i)), 2)

    for i in range(BOXES + 1):
        for f, value in enumerate(z_faces(0, i, fields(0, i))):
            low_faces[f, i] = value

    def fill_out(z, carry):
        below = [pltpu.roll(f, 1, 0) for f in x_faces(z, chunks - 1, fields(z, chunks - 1))]
        uppers, finals = [], []
        for i in range(BOXES + 1):
            u = fields(z, i)
            flux = x_faces(z, i, u)
            turned = [pltpu.roll(f, 1, 0) for f in flux]
            total = []
            for f in range(6):
                lower = jnp.where(row == 0, below[f], turned[f])
                total.append(pltpu.roll(jnp.where(lane >= LANES - BW, lower, flux[f]), BW, 1) - flux[f])
            below = turned
            flux = y_faces(z, i, u)
            total = [t + (beside_y(f, BW - 1) - f) for t, f in zip(total, flux)]
            flux = z_faces(z, i, u)
            uppers.append(flux)
            finals.append([
                0.5 * (u_ref[f, z, pl.ds(8 * i, 8)] + u[f]) + half_step * (total[f] + (low_faces[f, i] - flux[f]))
                for f in range(6)
            ])
        for i in range(BOXES + 1):
            for f in range(6):
                low_faces[f, i] = uppers[i][f]
                if i < BOXES:
                    value = jnp.where(leaving, finals[i + 1][f], finals[i][f])
                    value = jnp.where(emptied, 0.0, value) if i == BOXES - 1 else value
                else:
                    value = jnp.where(filled, finals[i][f], 0.0)
                out_ref[f, pl.ds(i * 8 * DEPTH + z - 1, 8, stride=DEPTH)] = value
        return carry

    lax.fori_loop(1, 5, fill_out, 0)


def local(n_curve, n_near, primitive, conductivity, new_owner):
    rows = OWN * DEPTH
    prim = primitive.reshape(6, DEPTH, OWN, LANES).transpose(0, 2, 1, 3).reshape(6, rows, LANES)
    cond = conductivity.reshape(DEPTH, OWN, LANES).transpose(1, 0, 2).reshape(rows, LANES)
    n_y, n_z = Y_CHIPS, n_curve // Y_CHIPS
    hbm = pl.BlockSpec(memory_space=pltpu.HBM)
    vmem = pl.BlockSpec(memory_space=pltpu.VMEM)
    dma = pltpu.SemaphoreType.DMA
    state = pl.pallas_call(
        functools.partial(exchange_kernel, n_curve, n_near),
        out_shape=(
            pltpu.VMEM((7, 6, ROWS, LANES), F32),
            pltpu.VMEM((6, 6, ROWS, LANES), F32),
            pltpu.VMEM((2, 7, DEPTH, ROWS, LANES), F32),
            pltpu.VMEM((2, 6, DEPTH, ROWS, LANES), F32),
            pltpu.VMEM((1, LANES), F32),
            pltpu.VMEM((2, LANES), F32),
        ),
        in_specs=[hbm] * 3,
        out_specs=(vmem,) * 6,
        scratch_shapes=[
            pltpu.VMEM((7, rows, LANES), F32),
            pltpu.VMEM((7, NEXT, LANES), F32),
            pltpu.VMEM((7, PREV, LANES), F32),
            pltpu.VMEM((7, 8, ROWS, LANES), F32),
            pltpu.VMEM((6, 8, ROWS, LANES), F32),
            pltpu.VMEM((7, 2, ROWS, LANES), F32),
            pltpu.VMEM((7, 2, ROWS, LANES), F32),
            pltpu.VMEM((2, 1, LANES), F32),
            pltpu.VMEM((max(n_near * n_y - 1, 2 * n_z - 1), 1, LANES), F32),
            pltpu.VMEM((n_z, 1, LANES), F32),
            pltpu.VMEM((1, LANES), F32),
            pltpu.VMEM((1, LANES), F32),
            pltpu.SMEM((BOXES,), jnp.int32),
            dma((3,)),
            dma((2,)),
            dma((2,)),
            dma((5,)),
            dma((5,)),
            pltpu.SemaphoreType.REGULAR,
        ],
        compiler_params=pltpu.CompilerParams(collective_id=0, has_side_effects=True, vmem_limit_bytes=VMEM_LIMIT),
        name="exchange",
    )(*(pltpu.with_memory_space_constraint(v, pltpu.HBM) for v in (prim, cond, new_owner)))
    out = pl.pallas_call(
        finish_kernel,
        out_shape=jax.ShapeDtypeStruct((6, 32 * DEPTH, LANES), F32),
        in_specs=[vmem] * 6,
        out_specs=vmem,
        scratch_shapes=[
            pltpu.VMEM((6, 6, ROWS, LANES), F32),
            pltpu.VMEM((4, 6, ROWS, LANES), F32),
            pltpu.VMEM((6, BOXES + 1, 8, LANES), F32),
        ],
        compiler_params=pltpu.CompilerParams(vmem_limit_bytes=VMEM_LIMIT),
        name="finish",
    )(*(pltpu.with_memory_space_constraint(v, pltpu.VMEM) for v in state))
    out = out.reshape(6, 32, DEPTH, LANES).transpose(0, 2, 1, 3).reshape(6, DEPTH, 32 * LANES)
    return out[None]


def solution(mesh):
    n_curve, n_near = mesh.shape["curve"], mesh.shape["near"]
    return jax.shard_map(
        functools.partial(local, n_curve, n_near),
        mesh=mesh,
        in_specs=(P(None, "near", "curve"), P("near", "curve"), P("curve")),
        out_specs=P("curve", None, "near", None),
        check_vma=False,
    )
```

```python
import functools

import jax
import jax.numpy as jnp
from jax import lax
from jax.experimental import pallas as pl
from jax.experimental.pallas import tpu as pltpu
from jax.sharding import PartitionSpec as P

BW = 32
BOXES = 3
DEPTH = 4
LANES = 128
OWN = 24
ROWS = 40
NEXT = 40
PREV = 8
Y_CHIPS = 8
VMEM_LIMIT = 48 << 20
RELAY = 3
MESH = pl.DeviceIdType.MESH
F32 = jnp.float32


def lane_of(shape):
    return lax.broadcasted_iota(jnp.int32, shape, len(shape) - 1)


def row_of(shape):
    return lax.broadcasted_iota(jnp.int32, shape, 0)


def upper_y(v, ypos):
    return jnp.where(ypos == BW - 1, pltpu.roll(v, BW - 1, 1), pltpu.roll(v, LANES - 1, 1))


def lower_y(v, ypos):
    return jnp.where(ypos == 0, pltpu.roll(v, LANES - BW + 1, 1), pltpu.roll(v, 1, 1))


def upper_x(v, lane):
    above = pltpu.roll(v, v.shape[0] - 1, 0)
    return pltpu.roll(jnp.where(lane < BW, above, v), LANES - BW, 1)


def lower_x(v, lane):
    below = pltpu.roll(v, 1, 0)
    return pltpu.roll(jnp.where(lane >= LANES - BW, below, v), BW, 1)


def derive(cons):
    r, mx, my, mz, energy = cons[:5]
    inv = 1.0 / r
    vx, vy, vz = mx * inv, my * inv, mz * inv
    pressure = 0.4 * (energy - 0.5 * (mx * vx + my * vy + mz * vz))
    temp = pressure * inv
    return 0.5 * vx, 0.5 * vy, 0.5 * vz, 0.5 * jnp.sqrt(1.4 * temp), 0.5 * pressure, temp


def face(lo, hi, k):
    lu, ld, lc = lo
    hu, hd, hc = hi
    lw, hw = ld[k], hd[k]
    top = jnp.maximum(jnp.abs(lw) + ld[3], jnp.abs(hw) + hd[3])
    lf, hf = lw + top, hw - top
    flux = [a * lf + b * hf for a, b in zip(lu, hu)]
    flux[1 + k] = flux[1 + k] + (ld[4] + hd[4])
    work = ld[4] * lw + hd[4] * hw
    flux[4] = flux[4] + (work + work) - (lc + hc) * (hd[5] - ld[5])
    return flux


def mapped(cell, fn):
    u, d, c = cell
    return [fn(a) for a in u], [fn(a) for a in d], fn(c)


def plane_rate(get, z):
    mid = get(z)
    shape = mid[2].shape
    lane = lane_of(shape)
    ypos = lane % BW
    flux = face(mid, mapped(mid, lambda v: upper_x(v, lane)), 0)
    total = [lower_x(f, lane) - f for f in flux]
    flux = face(mid, mapped(mid, lambda v: upper_y(v, ypos)), 1)
    total = [t + (lower_y(f, ypos) - f) for t, f in zip(total, flux)]
    flux = face(mid, get(z + 1), 2)
    total = [t - f for t, f in zip(total, flux)]
    flux = face(get(z - 1), mid, 2)
    return [t + f for t, f in zip(total, flux)]


def spread(ref, f, row):
    return jnp.broadcast_to(ref[f, row : row + 1], (8, LANES))


def conserved(prim):
    r, vx, vy, vz, p, s = prim
    energy = p * 2.5 + 0.5 * r * (vx * vx + vy * vy + vz * vz)
    return r, r * vx, r * vy, r * vz, energy, r * s


def exchange_kernel(
    n_curve, n_near,
    prim_hbm, cond_hbm, owner_hbm,
    u_out, rate_out, u_side, rate_side, top_out, flag_out,
    raw, from_next, from_prev, ext, der, low_planes, high_planes,
    sent, got_plane, got_column, flag_sent, flag_got, owner,
    load_sem, stage_send, stage_recv, halo_send, halo_recv, relay,
):
    n_y, n_x = Y_CHIPS, n_near // 2
    n_z = n_curve // n_y
    curve, near = lax.axis_index("curve"), lax.axis_index("near")
    y, z_chip, x, core = lax.rem(curve, n_y), lax.div(curve, n_y), lax.div(near, 2), lax.rem(near, 2)
    first, last = curve == 0, curve == n_curve - 1
    loads = [
        pltpu.make_async_copy(prim_hbm, raw.at[pl.ds(0, 6)], load_sem.at[0]),
        pltpu.make_async_copy(cond_hbm, raw.at[6], load_sem.at[1]),
        pltpu.make_async_copy(owner_hbm, owner, load_sem.at[2]),
    ]
    for copy in loads:
        copy.start()

    def ring(j, n):
        return min(j % n, -j % n)

    ys = [lax.rem(y + j, n_y) for j in range(n_y)]
    xs = [2 * lax.rem(x + j, n_x) for j in range(n_x)]

    def plane_at(offset, side):
        return (n_y * z_chip + ys[offset[1]], xs[offset[0]] + side)

    def column_at(to, side):
        return (n_y * to + y, 2 * x + side)

    def for_close(act):
        for d in range(1, min(RELAY, n_z - 1) + 1):
            pl.when(z_chip >= d)(functools.partial(act, z_chip - d))
            pl.when(z_chip + d < n_z)(functools.partial(act, z_chip + d))

    plane = sorted(
        ((i, j) for i in range(n_x) for j in range(n_y)),
        key=lambda o: -ring(o[0], n_x) - ring(o[1], n_y),
    )
    slot_of = {o: o[0] * n_y + o[1] for o in plane}
    others = [o for o in plane if slot_of[o] > 0]
    n_plane = len(plane)
    before, after = (lax.rem(curve + n_curve - 1, n_curve), near), (lax.rem(curve + 1, n_curve), near)
    barrier = pltpu.get_barrier_semaphore()

    def greet(devices):
        for device in devices:
            pl.semaphore_signal(barrier, inc=1, device_id=device, device_id_type=MESH)

    @pl.when(core == 0)
    def _():
        greet([plane_at(o, 1) for o in plane])

    @pl.when(core == 1)
    def _():
        greet([plane_at(o, 1) for o in others] + [plane_at(o, 0) for o in plane])

    pl.when(jnp.logical_not(first))(lambda: greet([before]))
    pl.when(jnp.logical_not(last))(lambda: greet([after]))
    for_close(lambda to: greet([column_at(to, 1)]))

    for copy in loads:
        copy.wait()
    speed, cond = None, None
    for i in range(0, raw.shape[1], 8):
        r, vx, vy, vz, p = (raw[f, i : i + 8] for f in range(5))
        here = jnp.abs(vx) + jnp.abs(vy) + jnp.abs(vz) + 3.0 * jnp.sqrt(1.4 * p / r)
        k = raw[6, i : i + 8]
        speed = here if speed is None else jnp.maximum(speed, here)
        cond = k if cond is None else jnp.maximum(cond, k)
    lane8 = lane_of((8, LANES))
    both = jnp.where(
        lane8 < LANES // 2,
        jnp.maximum(speed, pltpu.roll(speed, LANES // 2, 1)),
        jnp.maximum(cond, pltpu.roll(cond, LANES // 2, 1)),
    )
    best = jnp.max(both, axis=0, keepdims=True)
    sent[0] = best
    leaving = jnp.where(owner[0] != curve, 1.0, 0.0).astype(F32)
    flag_sent[...] = jnp.full(flag_sent.shape, leaving, F32)

    def send(stage, got, slot, device):
        pltpu.make_async_remote_copy(
            src_ref=sent.at[stage], dst_ref=got.at[slot], send_sem=stage_send.at[stage],
            recv_sem=stage_recv.at[stage], device_id=device, device_id_type=MESH,
        ).start()

    def wait_rows(sem, got, count):
        rows = got.at[pl.ds(0, count)]
        pltpu.make_async_copy(rows, rows, sem).wait()

    def largest(rows):
        while len(rows) > 1:
            rows = [jnp.maximum(*rows[i : i + 2]) if i + 1 < len(rows) else rows[i] for i in range(0, len(rows), 2)]
        return rows[0]

    def halo(i, src, dst, device):
        return pltpu.make_async_remote_copy(
            src_ref=src, dst_ref=dst, send_sem=halo_send.at[i], recv_sem=halo_recv.at[i],
            device_id=device, device_id_type=MESH,
        )

    sides = lax.div(curve + n_curve - 1, n_curve) + 1 - lax.div(curve + 1, n_curve)
    contacts = 0
    for d in range(1, min(RELAY, n_z - 1) + 1):
        contacts = contacts + lax.div(z_chip - d + n_z, n_z) + 1 - lax.div(z_chip + d, n_z)

    @pl.when(core == 0)
    def _():
        pl.semaphore_wait(barrier, n_plane + sides)
        for o in plane:
            send(0, got_plane, n_plane - 1 + slot_of[o], plane_at(o, 1))

    @pl.when(core == 1)
    def _():
        pl.semaphore_wait(barrier, 2 * n_plane - 1 + 2 * contacts + sides)
        for o in others:
            send(0, got_plane, slot_of[o] - 1, plane_at(o, 1))

    def pass_on(sem, source, target):
        inside = (source >= 0, source < n_z), (target >= 0, target < n_z)
        pl.when(jnp.logical_and(*inside[0]))(lambda: pl.semaphore_wait(sem, 1))
        pl.when(jnp.logical_and(*inside[1]))(
            lambda: pl.semaphore_signal(sem, inc=1, device_id=column_at(target, 1), device_id_type=MESH)
        )

    def send_column(to):
        slot = lax.rem(to - z_chip + n_z, n_z)
        send(1, got_column, slot, column_at(to, 0))
        send(1, got_column, slot - 1, column_at(to, 1))

    def finish_column():
        pass_on(relay.at[1], z_chip + RELAY, z_chip - RELAY)

    def send_above():
        lax.fori_loop(z_chip + RELAY + 1, n_z, lambda to, c: (send_column(to), c)[1], 0)

    on_core = core == 1
    at_once = jnp.logical_and(on_core, z_chip + 2 * RELAY >= n_z)
    soon = jnp.logical_and(on_core, jnp.logical_and(z_chip >= RELAY, z_chip + 2 * RELAY < n_z))
    at_last = jnp.logical_and(on_core, jnp.logical_and(z_chip < RELAY, z_chip + 2 * RELAY < n_z))

    to_before = [halo(0, raw.at[:, pl.ds(0, NEXT)], from_next, before), halo(2, flag_sent, flag_got, before)]
    to_after = [halo(1, raw.at[:, pl.ds(raw.shape[1] - PREV, PREV)], from_prev, after)]

    @pl.when(jnp.logical_not(first))
    def _():
        for copy in to_before:
            copy.start()

    @pl.when(jnp.logical_not(last))
    def _():
        for copy in to_after:
            copy.start()

    pl.when(on_core)(lambda: pass_on(relay.at[0], z_chip - RELAY, z_chip + RELAY))
    pl.when(at_once)(finish_column)

    for z in range(DEPTH):
        for i in range(OWN // 8):
            rows = pl.ds(i * 8 * DEPTH + z, 8, stride=DEPTH)
            for f, value in enumerate(conserved([raw[f, rows] for f in range(6)])):
                ext[f, 2 + z, i * 8 : i * 8 + 8] = value
            ext[6, 2 + z, i * 8 : i * 8 + 8] = 0.5 * raw[6, rows]

    @pl.when(core == 1)
    def _():
        count = 2 * n_plane - 1
        wait_rows(stage_recv.at[0], got_plane, count)
        sent[1] = largest([sent[0]] + [got_plane[i] for i in range(count)])
        lax.fori_loop(0, z_chip, lambda to, c: (send_column(to), c)[1], 0)
        send(1, got_column, 0, column_at(z_chip, 0))
        for d in range(1, min(RELAY, n_z - 1) + 1):
            pl.when(z_chip + d < n_z)(functools.partial(send_column, z_chip + d))

    pl.when(at_once)(send_above)

    @pl.when(soon)
    def _():
        finish_column()
        send_above()

    row8 = row_of((8, LANES))

    @pl.when(jnp.logical_not(last))
    def _():
        for copy in to_before:
            copy.wait_recv()

    @pl.when(jnp.logical_not(first))
    def _():
        for copy in to_after:
            copy.wait_recv()

    for z in range(DEPTH):
        fourth, sides = [], []
        for f in range(7):
            v = from_next[f, pl.ds(z, 8, stride=DEPTH)]
            edge = pltpu.roll(spread(raw, f, (OWN - 1) * DEPTH + z), BW, 1)
            fourth.append(jnp.where(jnp.logical_and(last, row8 == 0), edge, v))
            after_row = spread(from_next, f, 8 * DEPTH + z)
            before_row = spread(from_prev, f, PREV - DEPTH + z)
            edge = pltpu.roll(spread(raw, f, z), LANES - BW, 1)
            before_row = jnp.where(first, edge, before_row)
            sides.append(jnp.where(row8 == 7, before_row, after_row))
        for i, group in ((OWN // 8, fourth), (OWN // 8 + 1, sides)):
            for f, value in enumerate(conserved(group[:6])):
                ext[f, 2 + z, i * 8 : i * 8 + 8] = value
            ext[6, 2 + z, i * 8 : i * 8 + 8] = 0.5 * group[6]

    plane_copies = [
        halo(3, ext.at[:, pl.ds(4, 2)], low_planes, (curve, lax.rem(near + 1, n_near))),
        halo(4, ext.at[:, pl.ds(2, 2)], high_planes, (curve, lax.rem(near + n_near - 1, n_near))),
    ]
    for copy in plane_copies:
        copy.start()

    def fill_derived(z):
        for i, value in enumerate(derive([ext[f, z] for f in range(5)])):
            der[i, z] = value

    def cell(z):
        return [ext[f, z] for f in range(6)], [der[i, z] for i in range(6)], ext[6, z]

    row = row_of((ROWS, LANES))
    left_edge = jnp.logical_and(first, row == ROWS - 1)
    right_edge = jnp.logical_and(last, row == OWN)

    def fill_rate(z):
        for f, value in enumerate(plane_rate(cell, z)):
            left = pltpu.roll(jnp.broadcast_to(value[0:1], value.shape), LANES - BW, 1)
            right = pltpu.roll(jnp.broadcast_to(value[OWN - 1 : OWN], value.shape), BW, 1)
            rate_out[f, z - 1] = jnp.where(right_edge, right, jnp.where(left_edge, left, value))

    def fill_sides(z):
        lane = lane_of((ROWS, LANES))
        for f in range(7):
            for ref, of in ((u_side, ext[f, z + 2]),) + (((rate_side, rate_out[f, z + 1]),) if f < 6 else ()):
                ref[0, f, z] = upper_x(of, lane)
                ref[1, f, z] = upper_y(of, lane % BW)

    lax.fori_loop(2, 6, lambda z, c: (fill_derived(z), c)[1], 0)

    lax.fori_loop(3, 5, lambda z, c: (fill_rate(z), c)[1], 0)

    for copy in plane_copies:
        copy.wait()
    for i in range(2):
        for f in range(7):
            ext[f, i] = low_planes[f, i]
            ext[f, 6 + i] = high_planes[f, i]
    for z in (0, 1, 6, 7):
        fill_derived(z)
    lax.fori_loop(0, 2, lambda i, c: (fill_rate(1 + 4 * i), c)[1], 0)
    lax.fori_loop(0, 2, lambda i, c: (fill_rate(2 + 4 * i), c)[1], 0)
    lax.fori_loop(0, DEPTH, lambda z, c: (fill_sides(z), c)[1], 0)
    for f in range(7):
        for z in range(6):
            u_out[f, z] = ext[f, z + 1]

    @pl.when(at_last)
    def _():
        finish_column()
        send_above()

    flag_out[0:1] = flag_sent[...]
    flag_out[1:2] = jnp.where(last, 0.0, flag_got[...])

    @pl.when(jnp.logical_not(first))
    def _():
        for copy in to_before:
            copy.wait_send()

    @pl.when(jnp.logical_not(last))
    def _():
        for copy in to_after:
            copy.wait_send()

    @pl.when(core == 0)
    def _():
        wait_rows(stage_send.at[0], got_plane, n_plane)
        wait_rows(stage_recv.at[1], got_column, n_z)
        top_out[...] = largest([got_column[i] for i in range(n_z)])

    @pl.when(core == 1)
    def _():
        wait_rows(stage_send.at[0], got_plane, n_plane - 1)
        wait_rows(stage_recv.at[1], got_column, n_z - 1)
        top_out[...] = largest([sent[1]] + [got_column[i] for i in range(n_z - 1)])
        wait_rows(stage_send.at[1], got_plane, 2 * n_z - 1)


def beside_y(v, by):
    lane = lane_of(v.shape)
    wanted = lane - lane % BW + (lane + by) % BW
    return jnp.take_along_axis(v, wanted, axis=1, mode="promise_in_bounds")


def with_pressure(u, w, c, k):
    temp = c * c
    return u, w, c, k, temp, u[0] * (temp * (0.5 / 0.35))


def second_face(lo, hi, k):
    (lu, lw, lc, lk, lt, lp), (hu, hw, hc, hk, ht, hp) = lo, hi
    top = jnp.maximum(jnp.abs(lw) + lc, jnp.abs(hw) + hc)
    lf, hf = lw + top, hw - top
    flux = [a * lf + b * hf for a, b in zip(lu, hu)]
    flux[1 + k] = flux[1 + k] + (lp + hp)
    work = lp * lw + hp * hw
    flux[4] = flux[4] + (work + work) - ((lk + hk) * (1.0 / 0.35)) * (ht - lt)
    return flux


def finish_kernel(u_ref, rate_ref, u_side, rate_side, top_ref, flag_ref, out_ref, half, der, low_faces):
    top = top_ref[...]
    lane = lane_of(top.shape)
    speed = jnp.max(jnp.where(lane < LANES // 2, top, 0.0), axis=1, keepdims=True)
    cond = jnp.max(jnp.where(lane < LANES // 2, 0.0, top), axis=1, keepdims=True)
    step = jnp.broadcast_to(0.8 / (speed + 6.0 * cond), (8, LANES))
    chunks = ROWS // 8
    lane, row = lane_of((8, LANES)), row_of((8, LANES))

    def fill_half(z, carry):
        for i in range(chunks):
            rows = pl.ds(8 * i, 8)
            values = [u_ref[f, z, rows] + step * rate_ref[f, z, rows] for f in range(6)]
            for f in range(6):
                half[f, z, rows] = values[f]
            for k, value in enumerate(derive(values[:5])[:4]):
                der[k, z, rows] = value
        return carry

    lax.fori_loop(0, 6, fill_half, 0)
    leaving = flag_ref[0:1] > 0.5
    arriving = flag_ref[1:2] > 0.5
    emptied = jnp.logical_and(leaving, jnp.logical_not(arriving))
    filled = jnp.logical_and(arriving, jnp.logical_not(leaving))
    half_step = 0.5 * step

    def fields(z, i):
        return [half[f, z, pl.ds(8 * i, 8)] for f in range(6)]

    def chunk(z, i, k, u):
        rows = pl.ds(8 * i, 8)
        return with_pressure(u, der[k, z, rows], der[3, z, rows], u_ref[6, z, rows])

    def side(k, z, i, w, c):
        rows = pl.ds(8 * i, 8)
        u = [u_side[k, f, z - 1, rows] + step * rate_side[k, f, z - 1, rows] for f in range(6)]
        return with_pressure(u, w, c, u_side[k, 6, z - 1, rows])

    def x_faces(z, i, u):
        def beside(k):
            if i == chunks - 1:
                above = jnp.broadcast_to(der[k, z, 0:1], (8, LANES))
            else:
                above = der[k, z, pl.ds(8 * i + 1, 8)]
            return pltpu.roll(jnp.where(lane < BW, above, der[k, z, pl.ds(8 * i, 8)]), LANES - BW, 1)

        return second_face(chunk(z, i, 0, u), side(0, z, i, beside(0), beside(3)), 0)

    def y_faces(z, i, u):
        rows = pl.ds(8 * i, 8)
        w, c = beside_y(der[1, z, rows], 1), beside_y(der[3, z, rows], 1)
        return second_face(chunk(z, i, 1, u), side(1, z, i, w, c), 1)

    def z_faces(z, i, u):
        return second_face(chunk(z, i, 2, u), chunk(z + 1, i, 2, fields(z + 1, i)), 2)

    for i in range(BOXES + 1):
        for f, value in enumerate(z_faces(0, i, fields(0, i))):
            low_faces[f, i] = value

    def fill_out(z, carry):
        below = [pltpu.roll(f, 1, 0) for f in x_faces(z, chunks - 1, fields(z, chunks - 1))]
        uppers, finals = [], []
        for i in range(BOXES + 1):
            u = fields(z, i)
            flux = x_faces(z, i, u)
            turned = [pltpu.roll(f, 1, 0) for f in flux]
            total = []
            for f in range(6):
                lower = jnp.where(row == 0, below[f], turned[f])
                total.append(pltpu.roll(jnp.where(lane >= LANES - BW, lower, flux[f]), BW, 1) - flux[f])
            below = turned
            flux = y_faces(z, i, u)
            total = [t + (beside_y(f, BW - 1) - f) for t, f in zip(total, flux)]
            flux = z_faces(z, i, u)
            uppers.append(flux)
            finals.append([
                0.5 * (u_ref[f, z, pl.ds(8 * i, 8)] + u[f]) + half_step * (total[f] + (low_faces[f, i] - flux[f]))
                for f in range(6)
            ])
        for i in range(BOXES + 1):
            for f in range(6):
                low_faces[f, i] = uppers[i][f]
                if i < BOXES:
                    value = jnp.where(leaving, finals[i + 1][f], finals[i][f])
                    value = jnp.where(emptied, 0.0, value) if i == BOXES - 1 else value
                else:
                    value = jnp.where(filled, finals[i][f], 0.0)
                out_ref[f, pl.ds(i * 8 * DEPTH + z - 1, 8, stride=DEPTH)] = value
        return carry

    lax.fori_loop(1, 5, fill_out, 0)


def local(n_curve, n_near, primitive, conductivity, new_owner):
    rows = OWN * DEPTH
    prim = primitive.reshape(6, DEPTH, OWN, LANES).transpose(0, 2, 1, 3).reshape(6, rows, LANES)
    cond = conductivity.reshape(DEPTH, OWN, LANES).transpose(1, 0, 2).reshape(rows, LANES)
    n_y, n_z = Y_CHIPS, n_curve // Y_CHIPS
    hbm = pl.BlockSpec(memory_space=pltpu.HBM)
    vmem = pl.BlockSpec(memory_space=pltpu.VMEM)
    dma = pltpu.SemaphoreType.DMA
    state = pl.pallas_call(
        functools.partial(exchange_kernel, n_curve, n_near),
        out_shape=(
            pltpu.VMEM((7, 6, ROWS, LANES), F32),
            pltpu.VMEM((6, 6, ROWS, LANES), F32),
            pltpu.VMEM((2, 7, DEPTH, ROWS, LANES), F32),
            pltpu.VMEM((2, 6, DEPTH, ROWS, LANES), F32),
            pltpu.VMEM((1, LANES), F32),
            pltpu.VMEM((2, LANES), F32),
        ),
        in_specs=[hbm] * 3,
        out_specs=(vmem,) * 6,
        scratch_shapes=[
            pltpu.VMEM((7, rows, LANES), F32),
            pltpu.VMEM((7, NEXT, LANES), F32),
            pltpu.VMEM((7, PREV, LANES), F32),
            pltpu.VMEM((7, 8, ROWS, LANES), F32),
            pltpu.VMEM((6, 8, ROWS, LANES), F32),
            pltpu.VMEM((7, 2, ROWS, LANES), F32),
            pltpu.VMEM((7, 2, ROWS, LANES), F32),
            pltpu.VMEM((2, 1, LANES), F32),
            pltpu.VMEM((max(n_near * n_y - 1, 2 * n_z - 1), 1, LANES), F32),
            pltpu.VMEM((n_z, 1, LANES), F32),
            pltpu.VMEM((1, LANES), F32),
            pltpu.VMEM((1, LANES), F32),
            pltpu.SMEM((BOXES,), jnp.int32),
            dma((3,)),
            dma((2,)),
            dma((2,)),
            dma((5,)),
            dma((5,)),
            pltpu.SemaphoreType.REGULAR((2,)),
        ],
        compiler_params=pltpu.CompilerParams(collective_id=0, has_side_effects=True, vmem_limit_bytes=VMEM_LIMIT),
        name="exchange",
    )(*(pltpu.with_memory_space_constraint(v, pltpu.HBM) for v in (prim, cond, new_owner)))
    out = pl.pallas_call(
        finish_kernel,
        out_shape=jax.ShapeDtypeStruct((6, 32 * DEPTH, LANES), F32),
        in_specs=[vmem] * 6,
        out_specs=vmem,
        scratch_shapes=[
            pltpu.VMEM((6, 6, ROWS, LANES), F32),
            pltpu.VMEM((4, 6, ROWS, LANES), F32),
            pltpu.VMEM((6, BOXES + 1, 8, LANES), F32),
        ],
        compiler_params=pltpu.CompilerParams(vmem_limit_bytes=VMEM_LIMIT),
        name="finish",
    )(*(pltpu.with_memory_space_constraint(v, pltpu.VMEM) for v in state))
    out = out.reshape(6, 32, DEPTH, LANES).transpose(0, 2, 1, 3).reshape(6, DEPTH, 32 * LANES)
    return out[None]


def solution(mesh):
    n_curve, n_near = mesh.shape["curve"], mesh.shape["near"]
    return jax.shard_map(
        functools.partial(local, n_curve, n_near),
        mesh=mesh,
        in_specs=(P(None, "near", "curve"), P("near", "curve"), P("curve")),
        out_specs=P("curve", None, "near", None),
        check_vma=False,
    )
```

```python
import functools

import jax
import jax.numpy as jnp
from jax import lax
from jax.experimental import pallas as pl
from jax.experimental.pallas import tpu as pltpu
from jax.sharding import PartitionSpec as P

BW = 32
BOXES = 3
DEPTH = 4
LANES = 128
OWN = 24
ROWS = 40
NEXT = 40
PREV = 8
Y_CHIPS = 8
VMEM_LIMIT = 48 << 20
RELAY = 3
MESH = pl.DeviceIdType.MESH
F32 = jnp.float32


def lane_of(shape):
    return lax.broadcasted_iota(jnp.int32, shape, len(shape) - 1)


def row_of(shape):
    return lax.broadcasted_iota(jnp.int32, shape, 0)


def upper_y(v, ypos):
    return jnp.where(ypos == BW - 1, pltpu.roll(v, BW - 1, 1), pltpu.roll(v, LANES - 1, 1))


def lower_y(v, ypos):
    return jnp.where(ypos == 0, pltpu.roll(v, LANES - BW + 1, 1), pltpu.roll(v, 1, 1))


def upper_x(v, lane):
    above = pltpu.roll(v, v.shape[0] - 1, 0)
    return pltpu.roll(jnp.where(lane < BW, above, v), LANES - BW, 1)


def lower_x(v, lane):
    below = pltpu.roll(v, 1, 0)
    return pltpu.roll(jnp.where(lane >= LANES - BW, below, v), BW, 1)


def derive(cons):
    r, mx, my, mz, energy = cons[:5]
    inv = 1.0 / r
    vx, vy, vz = mx * inv, my * inv, mz * inv
    pressure = 0.4 * (energy - 0.5 * (mx * vx + my * vy + mz * vz))
    temp = pressure * inv
    return 0.5 * vx, 0.5 * vy, 0.5 * vz, 0.5 * jnp.sqrt(1.4 * temp), 0.5 * pressure, temp


def face(lo, hi, k):
    lu, ld, lc = lo
    hu, hd, hc = hi
    lw, hw = ld[k], hd[k]
    top = jnp.maximum(jnp.abs(lw) + ld[3], jnp.abs(hw) + hd[3])
    lf, hf = lw + top, hw - top
    flux = [a * lf + b * hf for a, b in zip(lu, hu)]
    flux[1 + k] = flux[1 + k] + (ld[4] + hd[4])
    work = ld[4] * lw + hd[4] * hw
    flux[4] = flux[4] + (work + work) - (lc + hc) * (hd[5] - ld[5])
    return flux


def mapped(cell, fn):
    u, d, c = cell
    return [fn(a) for a in u], [fn(a) for a in d], fn(c)


def plane_rate(get, z):
    mid = get(z)
    shape = mid[2].shape
    lane = lane_of(shape)
    ypos = lane % BW
    flux = face(mid, mapped(mid, lambda v: upper_x(v, lane)), 0)
    total = [lower_x(f, lane) - f for f in flux]
    flux = face(mid, mapped(mid, lambda v: upper_y(v, ypos)), 1)
    total = [t + (lower_y(f, ypos) - f) for t, f in zip(total, flux)]
    flux = face(mid, get(z + 1), 2)
    total = [t - f for t, f in zip(total, flux)]
    flux = face(get(z - 1), mid, 2)
    return [t + f for t, f in zip(total, flux)]


def spread(ref, f, row):
    return jnp.broadcast_to(ref[f, row : row + 1], (8, LANES))


def conserved(prim):
    r, vx, vy, vz, p, s = prim
    energy = p * 2.5 + 0.5 * r * (vx * vx + vy * vy + vz * vz)
    return r, r * vx, r * vy, r * vz, energy, r * s


def exchange_kernel(
    n_curve, n_near,
    prim_hbm, cond_hbm, owner_hbm,
    u_out, rate_out, u_side, rate_side, top_out, flag_out,
    raw, from_next, from_prev, ext, der, low_planes, high_planes,
    sent, got_plane, got_column, flag_sent, flag_got, owner,
    load_sem, stage_send, stage_recv, halo_send, halo_recv, relay,
):
    n_y, n_x = Y_CHIPS, n_near // 2
    n_z = n_curve // n_y
    curve, near = lax.axis_index("curve"), lax.axis_index("near")
    y, z_chip, x, core = lax.rem(curve, n_y), lax.div(curve, n_y), lax.div(near, 2), lax.rem(near, 2)
    first, last = curve == 0, curve == n_curve - 1
    loads = [
        pltpu.make_async_copy(prim_hbm, raw.at[pl.ds(0, 6)], load_sem.at[0]),
        pltpu.make_async_copy(cond_hbm, raw.at[6], load_sem.at[1]),
        pltpu.make_async_copy(owner_hbm, owner, load_sem.at[2]),
    ]
    for copy in loads:
        copy.start()

    def ring(j, n):
        return min(j % n, -j % n)

    ys = [lax.rem(y + j, n_y) for j in range(n_y)]
    xs = [2 * lax.rem(x + j, n_x) for j in range(n_x)]

    def plane_at(offset, side):
        return (n_y * z_chip + ys[offset[1]], xs[offset[0]] + side)

    def column_at(to, side):
        return (n_y * to + y, 2 * x + side)

    def for_close(act):
        for d in range(1, min(RELAY, n_z - 1) + 1):
            pl.when(z_chip >= d)(functools.partial(act, z_chip - d))
            pl.when(z_chip + d < n_z)(functools.partial(act, z_chip + d))

    plane = sorted(
        ((i, j) for i in range(n_x) for j in range(n_y)),
        key=lambda o: -ring(o[0], n_x) - ring(o[1], n_y),
    )
    slot_of = {o: o[0] * n_y + o[1] for o in plane}
    others = [o for o in plane if slot_of[o] > 0]
    n_plane = len(plane)
    before, after = (lax.rem(curve + n_curve - 1, n_curve), near), (lax.rem(curve + 1, n_curve), near)
    barrier = pltpu.get_barrier_semaphore()

    def greet(devices):
        for device in devices:
            pl.semaphore_signal(barrier, inc=1, device_id=device, device_id_type=MESH)

    @pl.when(core == 0)
    def _():
        greet([plane_at(o, 1) for o in plane])

    @pl.when(core == 1)
    def _():
        greet([plane_at(o, side) for o in plane for side in (0, 1) if side == 0 or slot_of[o]])

    pl.when(jnp.logical_not(first))(lambda: greet([before]))
    pl.when(jnp.logical_not(last))(lambda: greet([after]))
    for_close(lambda to: greet([column_at(to, 1)]))

    for copy in loads:
        copy.wait()
    speed, cond = None, None
    for i in range(0, raw.shape[1], 8):
        r, vx, vy, vz, p = (raw[f, i : i + 8] for f in range(5))
        here = jnp.abs(vx) + jnp.abs(vy) + jnp.abs(vz) + 3.0 * jnp.sqrt(1.4 * p / r)
        k = raw[6, i : i + 8]
        speed = here if speed is None else jnp.maximum(speed, here)
        cond = k if cond is None else jnp.maximum(cond, k)
    lane8 = lane_of((8, LANES))
    both = jnp.where(
        lane8 < LANES // 2,
        jnp.maximum(speed, pltpu.roll(speed, LANES // 2, 1)),
        jnp.maximum(cond, pltpu.roll(cond, LANES // 2, 1)),
    )
    best = jnp.max(both, axis=0, keepdims=True)
    sent[0] = best
    leaving = jnp.where(owner[0] != curve, 1.0, 0.0).astype(F32)
    flag_sent[...] = jnp.full(flag_sent.shape, leaving, F32)

    def send(stage, got, slot, device):
        pltpu.make_async_remote_copy(
            src_ref=sent.at[stage], dst_ref=got.at[slot], send_sem=stage_send.at[stage],
            recv_sem=stage_recv.at[stage], device_id=device, device_id_type=MESH,
        ).start()

    def wait_rows(sem, got, count):
        rows = got.at[pl.ds(0, count)]
        pltpu.make_async_copy(rows, rows, sem).wait()

    def largest(rows):
        while len(rows) > 1:
            rows = [jnp.maximum(*rows[i : i + 2]) if i + 1 < len(rows) else rows[i] for i in range(0, len(rows), 2)]
        return rows[0]

    def halo(i, src, dst, device):
        return pltpu.make_async_remote_copy(
            src_ref=src, dst_ref=dst, send_sem=halo_send.at[i], recv_sem=halo_recv.at[i],
            device_id=device, device_id_type=MESH,
        )

    sides = lax.div(curve + n_curve - 1, n_curve) + 1 - lax.div(curve + 1, n_curve)
    contacts = 0
    for d in range(1, min(RELAY, n_z - 1) + 1):
        contacts = contacts + lax.div(z_chip - d + n_z, n_z) + 1 - lax.div(z_chip + d, n_z)

    @pl.when(core == 0)
    def _():
        pl.semaphore_wait(barrier, n_plane + sides)
        for o in plane:
            send(0, got_plane, n_plane - 1 + slot_of[o], plane_at(o, 1))

    @pl.when(core == 1)
    def _():
        pl.semaphore_wait(barrier, 2 * n_plane - 1 + 2 * contacts + sides)
        for o in others:
            send(0, got_plane, slot_of[o] - 1, plane_at(o, 1))

    def pass_on(sem, source, target):
        inside = (source >= 0, source < n_z), (target >= 0, target < n_z)
        pl.when(jnp.logical_and(*inside[0]))(lambda: pl.semaphore_wait(sem, 1))
        pl.when(jnp.logical_and(*inside[1]))(
            lambda: pl.semaphore_signal(sem, inc=1, device_id=column_at(target, 1), device_id_type=MESH)
        )

    def send_column(to):
        slot = lax.rem(to - z_chip + n_z, n_z)
        send(1, got_column, slot, column_at(to, 0))
        send(1, got_column, slot - 1, column_at(to, 1))

    def finish_column():
        pass_on(relay.at[1], z_chip + RELAY, z_chip - RELAY)

    def send_above():
        lax.fori_loop(z_chip + RELAY + 1, n_z, lambda to, c: (send_column(to), c)[1], 0)

    on_core = core == 1
    at_once = jnp.logical_and(on_core, z_chip + 2 * RELAY >= n_z)
    soon = jnp.logical_and(on_core, jnp.logical_and(z_chip >= RELAY, z_chip + 2 * RELAY < n_z))
    at_last = jnp.logical_and(on_core, jnp.logical_and(z_chip < RELAY, z_chip + 2 * RELAY < n_z))

    to_before = [halo(0, raw.at[:, pl.ds(0, NEXT)], from_next, before), halo(2, flag_sent, flag_got, before)]
    to_after = [halo(1, raw.at[:, pl.ds(raw.shape[1] - PREV, PREV)], from_prev, after)]

    @pl.when(jnp.logical_not(first))
    def _():
        for copy in to_before:
            copy.start()

    @pl.when(jnp.logical_not(last))
    def _():
        for copy in to_after:
            copy.start()

    pl.when(on_core)(lambda: pass_on(relay.at[0], z_chip - RELAY, z_chip + RELAY))
    pl.when(at_once)(finish_column)

    for z in range(DEPTH):
        for i in range(OWN // 8):
            rows = pl.ds(i * 8 * DEPTH + z, 8, stride=DEPTH)
            for f, value in enumerate(conserved([raw[f, rows] for f in range(6)])):
                ext[f, 2 + z, i * 8 : i * 8 + 8] = value
            ext[6, 2 + z, i * 8 : i * 8 + 8] = 0.5 * raw[6, rows]

    @pl.when(core == 1)
    def _():
        count = 2 * n_plane - 1
        wait_rows(stage_recv.at[0], got_plane, count)
        sent[1] = largest([sent[0]] + [got_plane[i] for i in range(count)])
        lax.fori_loop(0, z_chip, lambda to, c: (send_column(to), c)[1], 0)
        send(1, got_column, 0, column_at(z_chip, 0))
        for d in range(1, min(RELAY, n_z - 1) + 1):
            pl.when(z_chip + d < n_z)(functools.partial(send_column, z_chip + d))

    pl.when(at_once)(send_above)

    @pl.when(soon)
    def _():
        finish_column()
        send_above()

    row8 = row_of((8, LANES))

    @pl.when(jnp.logical_not(last))
    def _():
        for copy in to_before:
            copy.wait_recv()

    @pl.when(jnp.logical_not(first))
    def _():
        for copy in to_after:
            copy.wait_recv()

    for z in range(DEPTH):
        fourth, sides = [], []
        for f in range(7):
            v = from_next[f, pl.ds(z, 8, stride=DEPTH)]
            edge = pltpu.roll(spread(raw, f, (OWN - 1) * DEPTH + z), BW, 1)
            fourth.append(jnp.where(jnp.logical_and(last, row8 == 0), edge, v))
            after_row = spread(from_next, f, 8 * DEPTH + z)
            before_row = spread(from_prev, f, PREV - DEPTH + z)
            edge = pltpu.roll(spread(raw, f, z), LANES - BW, 1)
            before_row = jnp.where(first, edge, before_row)
            sides.append(jnp.where(row8 == 7, before_row, after_row))
        for i, group in ((OWN // 8, fourth), (OWN // 8 + 1, sides)):
            for f, value in enumerate(conserved(group[:6])):
                ext[f, 2 + z, i * 8 : i * 8 + 8] = value
            ext[6, 2 + z, i * 8 : i * 8 + 8] = 0.5 * group[6]

    plane_copies = [
        halo(3, ext.at[:, pl.ds(4, 2)], low_planes, (curve, lax.rem(near + 1, n_near))),
        halo(4, ext.at[:, pl.ds(2, 2)], high_planes, (curve, lax.rem(near + n_near - 1, n_near))),
    ]
    for copy in plane_copies:
        copy.start()

    def fill_derived(z):
        for i, value in enumerate(derive([ext[f, z] for f in range(5)])):
            der[i, z] = value

    def cell(z):
        return [ext[f, z] for f in range(6)], [der[i, z] for i in range(6)], ext[6, z]

    row = row_of((ROWS, LANES))
    left_edge = jnp.logical_and(first, row == ROWS - 1)
    right_edge = jnp.logical_and(last, row == OWN)

    def fill_rate(z):
        for f, value in enumerate(plane_rate(cell, z)):
            left = pltpu.roll(jnp.broadcast_to(value[0:1], value.shape), LANES - BW, 1)
            right = pltpu.roll(jnp.broadcast_to(value[OWN - 1 : OWN], value.shape), BW, 1)
            rate_out[f, z - 1] = jnp.where(right_edge, right, jnp.where(left_edge, left, value))

    def fill_sides(z):
        lane = lane_of((ROWS, LANES))
        for f in range(7):
            for ref, of in ((u_side, ext[f, z + 2]),) + (((rate_side, rate_out[f, z + 1]),) if f < 6 else ()):
                ref[0, f, z] = upper_x(of, lane)
                ref[1, f, z] = upper_y(of, lane % BW)

    lax.fori_loop(2, 6, lambda z, c: (fill_derived(z), c)[1], 0)

    lax.fori_loop(3, 5, lambda z, c: (fill_rate(z), c)[1], 0)

    for copy in plane_copies:
        copy.wait()
    for i in range(2):
        for f in range(7):
            ext[f, i] = low_planes[f, i]
            ext[f, 6 + i] = high_planes[f, i]
    for z in (0, 1, 6, 7):
        fill_derived(z)
    lax.fori_loop(0, 2, lambda i, c: (fill_rate(1 + 4 * i), c)[1], 0)
    lax.fori_loop(0, 2, lambda i, c: (fill_rate(2 + 4 * i), c)[1], 0)
    lax.fori_loop(0, DEPTH, lambda z, c: (fill_sides(z), c)[1], 0)
    for f in range(7):
        for z in range(6):
            u_out[f, z] = ext[f, z + 1]

    @pl.when(at_last)
    def _():
        finish_column()
        send_above()

    flag_out[0:1] = flag_sent[...]
    flag_out[1:2] = jnp.where(last, 0.0, flag_got[...])

    @pl.when(jnp.logical_not(first))
    def _():
        for copy in to_before:
            copy.wait_send()

    @pl.when(jnp.logical_not(last))
    def _():
        for copy in to_after:
            copy.wait_send()

    @pl.when(core == 0)
    def _():
        wait_rows(stage_send.at[0], got_plane, n_plane)
        wait_rows(stage_recv.at[1], got_column, n_z)
        top_out[...] = largest([got_column[i] for i in range(n_z)])

    @pl.when(core == 1)
    def _():
        wait_rows(stage_send.at[0], got_plane, n_plane - 1)
        wait_rows(stage_recv.at[1], got_column, n_z - 1)
        top_out[...] = largest([sent[1]] + [got_column[i] for i in range(n_z - 1)])
        wait_rows(stage_send.at[1], got_plane, 2 * n_z - 1)


def beside_y(v, by):
    lane = lane_of(v.shape)
    wanted = lane - lane % BW + (lane + by) % BW
    return jnp.take_along_axis(v, wanted, axis=1, mode="promise_in_bounds")


def with_pressure(u, w, c, k):
    temp = c * c
    return u, w, c, k, temp, u[0] * (temp * (0.5 / 0.35))


def second_face(lo, hi, k):
    (lu, lw, lc, lk, lt, lp), (hu, hw, hc, hk, ht, hp) = lo, hi
    top = jnp.maximum(jnp.abs(lw) + lc, jnp.abs(hw) + hc)
    lf, hf = lw + top, hw - top
    flux = [a * lf + b * hf for a, b in zip(lu, hu)]
    flux[1 + k] = flux[1 + k] + (lp + hp)
    work = lp * lw + hp * hw
    flux[4] = flux[4] + (work + work) - ((lk + hk) * (1.0 / 0.35)) * (ht - lt)
    return flux


def finish_kernel(u_ref, rate_ref, u_side, rate_side, top_ref, flag_ref, out_ref, half, der, low_faces):
    top = top_ref[...]
    lane = lane_of(top.shape)
    speed = jnp.max(jnp.where(lane < LANES // 2, top, 0.0), axis=1, keepdims=True)
    cond = jnp.max(jnp.where(lane < LANES // 2, 0.0, top), axis=1, keepdims=True)
    step = jnp.broadcast_to(0.8 / (speed + 6.0 * cond), (8, LANES))
    chunks = ROWS // 8
    lane, row = lane_of((8, LANES)), row_of((8, LANES))

    def fill_half(z, count):
        for i in range(count):
            rows = pl.ds(8 * i, 8)
            values = [u_ref[f, z, rows] + step * rate_ref[f, z, rows] for f in range(6)]
            for f in range(6):
                half[f, z, rows] = values[f]
            for k, value in enumerate(derive(values[:5])[:4]):
                der[k, z, rows] = value

    lax.fori_loop(0, 2, lambda j, c: (fill_half(5 * j, BOXES + 1), c)[1], 0)
    lax.fori_loop(1, 5, lambda z, c: (fill_half(z, chunks), c)[1], 0)
    leaving = flag_ref[0:1] > 0.5
    arriving = flag_ref[1:2] > 0.5
    emptied = jnp.logical_and(leaving, jnp.logical_not(arriving))
    filled = jnp.logical_and(arriving, jnp.logical_not(leaving))
    half_step = 0.5 * step

    def fields(z, i):
        return [half[f, z, pl.ds(8 * i, 8)] for f in range(6)]

    def chunk(z, i, k, u):
        rows = pl.ds(8 * i, 8)
        return with_pressure(u, der[k, z, rows], der[3, z, rows], u_ref[6, z, rows])

    def side(k, z, i, w, c):
        rows = pl.ds(8 * i, 8)
        u = [u_side[k, f, z - 1, rows] + step * rate_side[k, f, z - 1, rows] for f in range(6)]
        return with_pressure(u, w, c, u_side[k, 6, z - 1, rows])

    def x_faces(z, i, u):
        def beside(k):
            if i == chunks - 1:
                above = jnp.broadcast_to(der[k, z, 0:1], (8, LANES))
            else:
                above = der[k, z, pl.ds(8 * i + 1, 8)]
            return pltpu.roll(jnp.where(lane < BW, above, der[k, z, pl.ds(8 * i, 8)]), LANES - BW, 1)

        return second_face(chunk(z, i, 0, u), side(0, z, i, beside(0), beside(3)), 0)

    def y_faces(z, i, u):
        rows = pl.ds(8 * i, 8)
        w, c = beside_y(der[1, z, rows], 1), beside_y(der[3, z, rows], 1)
        return second_face(chunk(z, i, 1, u), side(1, z, i, w, c), 1)

    def z_faces(z, i, u):
        return second_face(chunk(z, i, 2, u), chunk(z + 1, i, 2, fields(z + 1, i)), 2)

    for i in range(BOXES + 1):
        for f, value in enumerate(z_faces(0, i, fields(0, i))):
            low_faces[f, i] = value

    def fill_out(z, carry):
        below = [pltpu.roll(f, 1, 0) for f in x_faces(z, chunks - 1, fields(z, chunks - 1))]
        uppers, finals = [], []
        for i in range(BOXES + 1):
            u = fields(z, i)
            flux = x_faces(z, i, u)
            turned = [pltpu.roll(f, 1, 0) for f in flux]
            total = []
            for f in range(6):
                lower = jnp.where(row == 0, below[f], turned[f])
                total.append(pltpu.roll(jnp.where(lane >= LANES - BW, lower, flux[f]), BW, 1) - flux[f])
            below = turned
            flux = y_faces(z, i, u)
            total = [t + (beside_y(f, BW - 1) - f) for t, f in zip(total, flux)]
            flux = z_faces(z, i, u)
            uppers.append(flux)
            finals.append([
                0.5 * (u_ref[f, z, pl.ds(8 * i, 8)] + u[f]) + half_step * (total[f] + (low_faces[f, i] - flux[f]))
                for f in range(6)
            ])
        for i in range(BOXES + 1):
            for f in range(6):
                low_faces[f, i] = uppers[i][f]
                if i < BOXES:
                    value = jnp.where(leaving, finals[i + 1][f], finals[i][f])
                    value = jnp.where(emptied, 0.0, value) if i == BOXES - 1 else value
                else:
                    value = jnp.where(filled, finals[i][f], 0.0)
                out_ref[f, pl.ds(i * 8 * DEPTH + z - 1, 8, stride=DEPTH)] = value
        return carry

    lax.fori_loop(1, 5, fill_out, 0)


def local(n_curve, n_near, primitive, conductivity, new_owner):
    rows = OWN * DEPTH
    prim = primitive.reshape(6, DEPTH, OWN, LANES).transpose(0, 2, 1, 3).reshape(6, rows, LANES)
    cond = conductivity.reshape(DEPTH, OWN, LANES).transpose(1, 0, 2).reshape(rows, LANES)
    n_y, n_z = Y_CHIPS, n_curve // Y_CHIPS
    hbm = pl.BlockSpec(memory_space=pltpu.HBM)
    vmem = pl.BlockSpec(memory_space=pltpu.VMEM)
    dma = pltpu.SemaphoreType.DMA
    state = pl.pallas_call(
        functools.partial(exchange_kernel, n_curve, n_near),
        out_shape=(
            pltpu.VMEM((7, 6, ROWS, LANES), F32),
            pltpu.VMEM((6, 6, ROWS, LANES), F32),
            pltpu.VMEM((2, 7, DEPTH, ROWS, LANES), F32),
            pltpu.VMEM((2, 6, DEPTH, ROWS, LANES), F32),
            pltpu.VMEM((1, LANES), F32),
            pltpu.VMEM((2, LANES), F32),
        ),
        in_specs=[hbm] * 3,
        out_specs=(vmem,) * 6,
        scratch_shapes=[
            pltpu.VMEM((7, rows, LANES), F32),
            pltpu.VMEM((7, NEXT, LANES), F32),
            pltpu.VMEM((7, PREV, LANES), F32),
            pltpu.VMEM((7, 8, ROWS, LANES), F32),
            pltpu.VMEM((6, 8, ROWS, LANES), F32),
            pltpu.VMEM((7, 2, ROWS, LANES), F32),
            pltpu.VMEM((7, 2, ROWS, LANES), F32),
            pltpu.VMEM((2, 1, LANES), F32),
            pltpu.VMEM((max(n_near * n_y - 1, 2 * n_z - 1), 1, LANES), F32),
            pltpu.VMEM((n_z, 1, LANES), F32),
            pltpu.VMEM((1, LANES), F32),
            pltpu.VMEM((1, LANES), F32),
            pltpu.SMEM((BOXES,), jnp.int32),
            dma((3,)),
            dma((2,)),
            dma((2,)),
            dma((5,)),
            dma((5,)),
            pltpu.SemaphoreType.REGULAR((2,)),
        ],
        compiler_params=pltpu.CompilerParams(collective_id=0, has_side_effects=True, vmem_limit_bytes=VMEM_LIMIT),
        name="exchange",
    )(*(pltpu.with_memory_space_constraint(v, pltpu.HBM) for v in (prim, cond, new_owner)))
    out = pl.pallas_call(
        finish_kernel,
        out_shape=jax.ShapeDtypeStruct((6, 32 * DEPTH, LANES), F32),
        in_specs=[vmem] * 6,
        out_specs=vmem,
        scratch_shapes=[
            pltpu.VMEM((6, 6, ROWS, LANES), F32),
            pltpu.VMEM((4, 6, ROWS, LANES), F32),
            pltpu.VMEM((6, BOXES + 1, 8, LANES), F32),
        ],
        compiler_params=pltpu.CompilerParams(vmem_limit_bytes=VMEM_LIMIT),
        name="finish",
    )(*(pltpu.with_memory_space_constraint(v, pltpu.VMEM) for v in state))
    out = out.reshape(6, 32, DEPTH, LANES).transpose(0, 2, 1, 3).reshape(6, DEPTH, 32 * LANES)
    return out[None]


def solution(mesh):
    n_curve, n_near = mesh.shape["curve"], mesh.shape["near"]
    return jax.shard_map(
        functools.partial(local, n_curve, n_near),
        mesh=mesh,
        in_specs=(P(None, "near", "curve"), P("near", "curve"), P("curve")),
        out_specs=P("curve", None, "near", None),
        check_vma=False,
    )
```

```python
import functools

import jax
import jax.numpy as jnp
from jax import lax
from jax.experimental import pallas as pl
from jax.experimental.pallas import tpu as pltpu
from jax.sharding import PartitionSpec as P

BW = 32
BOXES = 3
DEPTH = 4
LANES = 128
OWN = 24
ROWS = 40
NEXT = 40
PREV = 8
Y_CHIPS = 8
VMEM_LIMIT = 48 << 20
RELAY = 3
MESH = pl.DeviceIdType.MESH
F32 = jnp.float32


def lane_of(shape):
    return lax.broadcasted_iota(jnp.int32, shape, len(shape) - 1)


def row_of(shape):
    return lax.broadcasted_iota(jnp.int32, shape, 0)


def upper_y(v, ypos):
    return jnp.where(ypos == BW - 1, pltpu.roll(v, BW - 1, 1), pltpu.roll(v, LANES - 1, 1))


def lower_y(v, ypos):
    return jnp.where(ypos == 0, pltpu.roll(v, LANES - BW + 1, 1), pltpu.roll(v, 1, 1))


def upper_x(v, lane):
    above = pltpu.roll(v, v.shape[0] - 1, 0)
    return pltpu.roll(jnp.where(lane < BW, above, v), LANES - BW, 1)


def lower_x(v, lane):
    below = pltpu.roll(v, 1, 0)
    return pltpu.roll(jnp.where(lane >= LANES - BW, below, v), BW, 1)


def derive(cons):
    r, mx, my, mz, energy = cons[:5]
    inv = 1.0 / r
    vx, vy, vz = mx * inv, my * inv, mz * inv
    pressure = 0.4 * (energy - 0.5 * (mx * vx + my * vy + mz * vz))
    temp = pressure * inv
    return 0.5 * vx, 0.5 * vy, 0.5 * vz, 0.5 * jnp.sqrt(1.4 * temp), 0.5 * pressure, temp


def face(lo, hi, k):
    lu, ld, lc = lo
    hu, hd, hc = hi
    lw, hw = ld[k], hd[k]
    top = jnp.maximum(jnp.abs(lw) + ld[3], jnp.abs(hw) + hd[3])
    lf, hf = lw + top, hw - top
    flux = [a * lf + b * hf for a, b in zip(lu, hu)]
    flux[1 + k] = flux[1 + k] + (ld[4] + hd[4])
    work = ld[4] * lw + hd[4] * hw
    flux[4] = flux[4] + (work + work) - (lc + hc) * (hd[5] - ld[5])
    return flux


def mapped(cell, fn):
    u, d, c = cell
    return [fn(a) for a in u], [fn(a) for a in d], fn(c)


def plane_rate(get, z):
    mid = get(z)
    shape = mid[2].shape
    lane = lane_of(shape)
    ypos = lane % BW
    flux = face(mid, mapped(mid, lambda v: upper_x(v, lane)), 0)
    total = [lower_x(f, lane) - f for f in flux]
    flux = face(mid, mapped(mid, lambda v: upper_y(v, ypos)), 1)
    total = [t + (lower_y(f, ypos) - f) for t, f in zip(total, flux)]
    flux = face(mid, get(z + 1), 2)
    total = [t - f for t, f in zip(total, flux)]
    flux = face(get(z - 1), mid, 2)
    return [t + f for t, f in zip(total, flux)]


def spread(ref, f, row):
    return jnp.broadcast_to(ref[f, row : row + 1], (8, LANES))


def conserved(prim):
    r, vx, vy, vz, p, s = prim
    energy = p * 2.5 + 0.5 * r * (vx * vx + vy * vy + vz * vz)
    return r, r * vx, r * vy, r * vz, energy, r * s


def exchange_kernel(
    n_curve, n_near,
    prim_hbm, cond_hbm, owner_hbm,
    u_out, rate_out, u_side, rate_side, top_out, flag_out,
    raw, from_next, from_prev, ext, der, low_planes, high_planes,
    sent, got_plane, got_column, flag_sent, flag_got, owner,
    load_sem, stage_send, stage_recv, halo_send, halo_recv, relay,
):
    n_y, n_x = Y_CHIPS, n_near // 2
    n_z = n_curve // n_y
    curve, near = lax.axis_index("curve"), lax.axis_index("near")
    y, z_chip, x, core = lax.rem(curve, n_y), lax.div(curve, n_y), lax.div(near, 2), lax.rem(near, 2)
    first, last = curve == 0, curve == n_curve - 1
    loads = [
        pltpu.make_async_copy(prim_hbm, raw.at[pl.ds(0, 6)], load_sem.at[0]),
        pltpu.make_async_copy(cond_hbm, raw.at[6], load_sem.at[1]),
        pltpu.make_async_copy(owner_hbm, owner, load_sem.at[2]),
    ]
    for copy in loads:
        copy.start()

    def ring(j, n):
        return min(j % n, -j % n)

    ys = [lax.rem(y + j, n_y) for j in range(n_y)]
    xs = [2 * lax.rem(x + j, n_x) for j in range(n_x)]

    def plane_at(offset, side):
        return (n_y * z_chip + ys[offset[1]], xs[offset[0]] + side)

    def column_at(to, side):
        return (n_y * to + y, 2 * x + side)

    def for_close(act):
        for d in range(1, min(RELAY, n_z - 1) + 1):
            pl.when(z_chip >= d)(functools.partial(act, z_chip - d))
            pl.when(z_chip + d < n_z)(functools.partial(act, z_chip + d))

    plane = sorted(
        ((i, j) for i in range(n_x) for j in range(n_y)),
        key=lambda o: -ring(o[0], n_x) - ring(o[1], n_y),
    )
    slot_of = {o: o[0] * n_y + o[1] for o in plane}
    others = [o for o in plane if slot_of[o] > 0]
    n_plane = len(plane)
    before, after = (lax.rem(curve + n_curve - 1, n_curve), near), (lax.rem(curve + 1, n_curve), near)
    barrier = pltpu.get_barrier_semaphore()

    def greet(devices):
        for device in devices:
            pl.semaphore_signal(barrier, inc=1, device_id=device, device_id_type=MESH)

    @pl.when(core == 0)
    def _():
        greet([plane_at(o, 1) for o in plane])

    @pl.when(core == 1)
    def _():
        greet([plane_at(o, 1) for o in others] + [plane_at(o, 0) for o in plane])

    pl.when(jnp.logical_not(first))(lambda: greet([before]))
    pl.when(jnp.logical_not(last))(lambda: greet([after]))
    for_close(lambda to: greet([column_at(to, 1)]))

    for copy in loads[:2]:
        copy.wait()
    speed, cond = None, None
    for i in range(0, raw.shape[1], 8):
        r, vx, vy, vz, p = (raw[f, i : i + 8] for f in range(5))
        here = jnp.abs(vx) + jnp.abs(vy) + jnp.abs(vz) + 3.0 * jnp.sqrt(1.4 * p / r)
        k = raw[6, i : i + 8]
        speed = here if speed is None else jnp.maximum(speed, here)
        cond = k if cond is None else jnp.maximum(cond, k)
    lane8 = lane_of((8, LANES))
    both = jnp.where(
        lane8 < LANES // 2,
        jnp.maximum(speed, pltpu.roll(speed, LANES // 2, 1)),
        jnp.maximum(cond, pltpu.roll(cond, LANES // 2, 1)),
    )
    best = jnp.max(both, axis=0, keepdims=True)
    sent[0] = best

    def send(stage, got, slot, device):
        pltpu.make_async_remote_copy(
            src_ref=sent.at[stage], dst_ref=got.at[slot], send_sem=stage_send.at[stage],
            recv_sem=stage_recv.at[stage], device_id=device, device_id_type=MESH,
        ).start()

    def wait_rows(sem, got, count):
        rows = got.at[pl.ds(0, count)]
        pltpu.make_async_copy(rows, rows, sem).wait()

    def largest(rows):
        while len(rows) > 1:
            rows = [jnp.maximum(*rows[i : i + 2]) if i + 1 < len(rows) else rows[i] for i in range(0, len(rows), 2)]
        return rows[0]

    def halo(i, src, dst, device):
        return pltpu.make_async_remote_copy(
            src_ref=src, dst_ref=dst, send_sem=halo_send.at[i], recv_sem=halo_recv.at[i],
            device_id=device, device_id_type=MESH,
        )

    sides = lax.div(curve + n_curve - 1, n_curve) + 1 - lax.div(curve + 1, n_curve)
    contacts = 0
    for d in range(1, min(RELAY, n_z - 1) + 1):
        contacts = contacts + lax.div(z_chip - d + n_z, n_z) + 1 - lax.div(z_chip + d, n_z)

    @pl.when(core == 0)
    def _():
        pl.semaphore_wait(barrier, n_plane + sides)
        for o in plane:
            send(0, got_plane, n_plane - 1 + slot_of[o], plane_at(o, 1))

    @pl.when(core == 1)
    def _():
        pl.semaphore_wait(barrier, 2 * n_plane - 1 + 2 * contacts + sides)
        for o in others:
            send(0, got_plane, slot_of[o] - 1, plane_at(o, 1))

    def pass_on(sem, source, target):
        inside = (source >= 0, source < n_z), (target >= 0, target < n_z)
        pl.when(jnp.logical_and(*inside[0]))(lambda: pl.semaphore_wait(sem, 1))
        pl.when(jnp.logical_and(*inside[1]))(
            lambda: pl.semaphore_signal(sem, inc=1, device_id=column_at(target, 1), device_id_type=MESH)
        )

    def send_column(to):
        slot = lax.rem(to - z_chip + n_z, n_z)
        send(1, got_column, slot, column_at(to, 0))
        send(1, got_column, slot - 1, column_at(to, 1))

    def finish_column():
        pass_on(relay.at[1], z_chip + RELAY, z_chip - RELAY)

    def send_above():
        lax.fori_loop(z_chip + RELAY + 1, n_z, lambda to, c: (send_column(to), c)[1], 0)

    on_core = core == 1
    at_once = jnp.logical_and(on_core, z_chip + 2 * RELAY >= n_z)
    soon = jnp.logical_and(on_core, jnp.logical_and(z_chip >= RELAY, z_chip + 2 * RELAY < n_z))
    at_last = jnp.logical_and(on_core, jnp.logical_and(z_chip < RELAY, z_chip + 2 * RELAY < n_z))

    loads[2].wait()
    leaving = jnp.where(owner[0] != curve, 1.0, 0.0).astype(F32)
    flag_sent[...] = jnp.full(flag_sent.shape, leaving, F32)
    to_before = [halo(0, raw.at[:, pl.ds(0, NEXT)], from_next, before), halo(2, flag_sent, flag_got, before)]
    to_after = [halo(1, raw.at[:, pl.ds(raw.shape[1] - PREV, PREV)], from_prev, after)]

    @pl.when(jnp.logical_not(first))
    def _():
        for copy in to_before:
            copy.start()

    @pl.when(jnp.logical_not(last))
    def _():
        for copy in to_after:
            copy.start()

    pl.when(on_core)(lambda: pass_on(relay.at[0], z_chip - RELAY, z_chip + RELAY))
    pl.when(at_once)(finish_column)

    for z in range(DEPTH):
        for i in range(OWN // 8):
            rows = pl.ds(i * 8 * DEPTH + z, 8, stride=DEPTH)
            for f, value in enumerate(conserved([raw[f, rows] for f in range(6)])):
                ext[f, 2 + z, i * 8 : i * 8 + 8] = value
            ext[6, 2 + z, i * 8 : i * 8 + 8] = 0.5 * raw[6, rows]

    @pl.when(core == 1)
    def _():
        count = 2 * n_plane - 1
        wait_rows(stage_recv.at[0], got_plane, count)
        sent[1] = largest([sent[0]] + [got_plane[i] for i in range(count)])
        lax.fori_loop(0, z_chip, lambda to, c: (send_column(to), c)[1], 0)
        send(1, got_column, 0, column_at(z_chip, 0))
        for d in range(1, min(RELAY, n_z - 1) + 1):
            pl.when(z_chip + d < n_z)(functools.partial(send_column, z_chip + d))

    pl.when(at_once)(send_above)

    @pl.when(soon)
    def _():
        finish_column()
        send_above()

    row8 = row_of((8, LANES))

    @pl.when(jnp.logical_not(last))
    def _():
        for copy in to_before:
            copy.wait_recv()

    @pl.when(jnp.logical_not(first))
    def _():
        for copy in to_after:
            copy.wait_recv()

    for z in range(DEPTH):
        fourth, sides = [], []
        for f in range(7):
            v = from_next[f, pl.ds(z, 8, stride=DEPTH)]
            edge = pltpu.roll(spread(raw, f, (OWN - 1) * DEPTH + z), BW, 1)
            fourth.append(jnp.where(jnp.logical_and(last, row8 == 0), edge, v))
            after_row = spread(from_next, f, 8 * DEPTH + z)
            before_row = spread(from_prev, f, PREV - DEPTH + z)
            edge = pltpu.roll(spread(raw, f, z), LANES - BW, 1)
            before_row = jnp.where(first, edge, before_row)
            sides.append(jnp.where(row8 == 7, before_row, after_row))
        for i, group in ((OWN // 8, fourth), (OWN // 8 + 1, sides)):
            for f, value in enumerate(conserved(group[:6])):
                ext[f, 2 + z, i * 8 : i * 8 + 8] = value
            ext[6, 2 + z, i * 8 : i * 8 + 8] = 0.5 * group[6]

    plane_copies = [
        halo(3, ext.at[:, pl.ds(4, 2)], low_planes, (curve, lax.rem(near + 1, n_near))),
        halo(4, ext.at[:, pl.ds(2, 2)], high_planes, (curve, lax.rem(near + n_near - 1, n_near))),
    ]
    for copy in plane_copies:
        copy.start()

    def fill_derived(z):
        for i, value in enumerate(derive([ext[f, z] for f in range(5)])):
            der[i, z] = value

    def cell(z):
        return [ext[f, z] for f in range(6)], [der[i, z] for i in range(6)], ext[6, z]

    row = row_of((ROWS, LANES))
    left_edge = jnp.logical_and(first, row == ROWS - 1)
    right_edge = jnp.logical_and(last, row == OWN)

    def fill_rate(z):
        for f, value in enumerate(plane_rate(cell, z)):
            left = pltpu.roll(jnp.broadcast_to(value[0:1], value.shape), LANES - BW, 1)
            right = pltpu.roll(jnp.broadcast_to(value[OWN - 1 : OWN], value.shape), BW, 1)
            rate_out[f, z - 1] = jnp.where(right_edge, right, jnp.where(left_edge, left, value))

    def fill_sides(z):
        lane = lane_of((ROWS, LANES))
        for f in range(7):
            for ref, of in ((u_side, ext[f, z + 2]),) + (((rate_side, rate_out[f, z + 1]),) if f < 6 else ()):
                ref[0, f, z] = upper_x(of, lane)
                ref[1, f, z] = upper_y(of, lane % BW)

    lax.fori_loop(2, 6, lambda z, c: (fill_derived(z), c)[1], 0)

    lax.fori_loop(3, 5, lambda z, c: (fill_rate(z), c)[1], 0)

    for copy in plane_copies:
        copy.wait()
    for i in range(2):
        for f in range(7):
            ext[f, i] = low_planes[f, i]
            ext[f, 6 + i] = high_planes[f, i]
    for z in (0, 1, 6, 7):
        fill_derived(z)
    lax.fori_loop(0, 2, lambda i, c: (fill_rate(1 + 4 * i), c)[1], 0)
    lax.fori_loop(0, 2, lambda i, c: (fill_rate(2 + 4 * i), c)[1], 0)
    lax.fori_loop(0, DEPTH, lambda z, c: (fill_sides(z), c)[1], 0)
    for f in range(7):
        for z in range(6):
            u_out[f, z] = ext[f, z + 1]

    @pl.when(at_last)
    def _():
        finish_column()
        send_above()

    flag_out[0:1] = flag_sent[...]
    flag_out[1:2] = jnp.where(last, 0.0, flag_got[...])

    @pl.when(jnp.logical_not(first))
    def _():
        for copy in to_before:
            copy.wait_send()

    @pl.when(jnp.logical_not(last))
    def _():
        for copy in to_after:
            copy.wait_send()

    @pl.when(core == 0)
    def _():
        wait_rows(stage_send.at[0], got_plane, n_plane)
        wait_rows(stage_recv.at[1], got_column, n_z)
        top_out[...] = largest([got_column[i] for i in range(n_z)])

    @pl.when(core == 1)
    def _():
        wait_rows(stage_send.at[0], got_plane, n_plane - 1)
        wait_rows(stage_recv.at[1], got_column, n_z - 1)
        top_out[...] = largest([sent[1]] + [got_column[i] for i in range(n_z - 1)])
        wait_rows(stage_send.at[1], got_plane, 2 * n_z - 1)


def beside_y(v, by):
    lane = lane_of(v.shape)
    wanted = lane - lane % BW + (lane + by) % BW
    return jnp.take_along_axis(v, wanted, axis=1, mode="promise_in_bounds")


def with_pressure(u, w, c, k):
    temp = c * c
    return u, w, c, k, temp, u[0] * (temp * (0.5 / 0.35))


def second_face(lo, hi, k):
    (lu, lw, lc, lk, lt, lp), (hu, hw, hc, hk, ht, hp) = lo, hi
    top = jnp.maximum(jnp.abs(lw) + lc, jnp.abs(hw) + hc)
    lf, hf = lw + top, hw - top
    flux = [a * lf + b * hf for a, b in zip(lu, hu)]
    flux[1 + k] = flux[1 + k] + (lp + hp)
    work = lp * lw + hp * hw
    flux[4] = flux[4] + (work + work) - ((lk + hk) * (1.0 / 0.35)) * (ht - lt)
    return flux


def finish_kernel(u_ref, rate_ref, u_side, rate_side, top_ref, flag_ref, out_ref, half, der, low_faces):
    top = top_ref[...]
    lane = lane_of(top.shape)
    speed = jnp.max(jnp.where(lane < LANES // 2, top, 0.0), axis=1, keepdims=True)
    cond = jnp.max(jnp.where(lane < LANES // 2, 0.0, top), axis=1, keepdims=True)
    step = jnp.broadcast_to(0.8 / (speed + 6.0 * cond), (8, LANES))
    chunks = ROWS // 8
    lane, row = lane_of((8, LANES)), row_of((8, LANES))

    def fill_half(z, carry):
        for i in range(chunks):
            rows = pl.ds(8 * i, 8)
            values = [u_ref[f, z, rows] + step * rate_ref[f, z, rows] for f in range(6)]
            for f in range(6):
                half[f, z, rows] = values[f]
            for k, value in enumerate(derive(values[:5])[:4]):
                der[k, z, rows] = value
        return carry

    lax.fori_loop(0, 6, fill_half, 0)
    leaving = flag_ref[0:1] > 0.5
    arriving = flag_ref[1:2] > 0.5
    emptied = jnp.logical_and(leaving, jnp.logical_not(arriving))
    filled = jnp.logical_and(arriving, jnp.logical_not(leaving))
    half_step = 0.5 * step

    def fields(z, i):
        return [half[f, z, pl.ds(8 * i, 8)] for f in range(6)]

    def chunk(z, i, k, u):
        rows = pl.ds(8 * i, 8)
        return with_pressure(u, der[k, z, rows], der[3, z, rows], u_ref[6, z, rows])

    def side(k, z, i, w, c):
        rows = pl.ds(8 * i, 8)
        u = [u_side[k, f, z - 1, rows] + step * rate_side[k, f, z - 1, rows] for f in range(6)]
        return with_pressure(u, w, c, u_side[k, 6, z - 1, rows])

    def x_faces(z, i, u):
        def beside(k):
            if i == chunks - 1:
                above = jnp.broadcast_to(der[k, z, 0:1], (8, LANES))
            else:
                above = der[k, z, pl.ds(8 * i + 1, 8)]
            return pltpu.roll(jnp.where(lane < BW, above, der[k, z, pl.ds(8 * i, 8)]), LANES - BW, 1)

        return second_face(chunk(z, i, 0, u), side(0, z, i, beside(0), beside(3)), 0)

    def y_faces(z, i, u):
        rows = pl.ds(8 * i, 8)
        w, c = beside_y(der[1, z, rows], 1), beside_y(der[3, z, rows], 1)
        return second_face(chunk(z, i, 1, u), side(1, z, i, w, c), 1)

    def z_faces(z, i, u):
        return second_face(chunk(z, i, 2, u), chunk(z + 1, i, 2, fields(z + 1, i)), 2)

    for i in range(BOXES + 1):
        for f, value in enumerate(z_faces(0, i, fields(0, i))):
            low_faces[f, i] = value

    def fill_out(z, carry):
        below = [pltpu.roll(f, 1, 0) for f in x_faces(z, chunks - 1, fields(z, chunks - 1))]
        uppers, finals = [], []
        for i in range(BOXES + 1):
            u = fields(z, i)
            flux = x_faces(z, i, u)
            turned = [pltpu.roll(f, 1, 0) for f in flux]
            total = []
            for f in range(6):
                lower = jnp.where(row == 0, below[f], turned[f])
                total.append(pltpu.roll(jnp.where(lane >= LANES - BW, lower, flux[f]), BW, 1) - flux[f])
            below = turned
            flux = y_faces(z, i, u)
            total = [t + (beside_y(f, BW - 1) - f) for t, f in zip(total, flux)]
            flux = z_faces(z, i, u)
            uppers.append(flux)
            finals.append([
                0.5 * (u_ref[f, z, pl.ds(8 * i, 8)] + u[f]) + half_step * (total[f] + (low_faces[f, i] - flux[f]))
                for f in range(6)
            ])
        for i in range(BOXES + 1):
            for f in range(6):
                low_faces[f, i] = uppers[i][f]
                if i < BOXES:
                    value = jnp.where(leaving, finals[i + 1][f], finals[i][f])
                    value = jnp.where(emptied, 0.0, value) if i == BOXES - 1 else value
                else:
                    value = jnp.where(filled, finals[i][f], 0.0)
                out_ref[f, pl.ds(i * 8 * DEPTH + z - 1, 8, stride=DEPTH)] = value
        return carry

    lax.fori_loop(1, 5, fill_out, 0)


def local(n_curve, n_near, primitive, conductivity, new_owner):
    rows = OWN * DEPTH
    prim = primitive.reshape(6, DEPTH, OWN, LANES).transpose(0, 2, 1, 3).reshape(6, rows, LANES)
    cond = conductivity.reshape(DEPTH, OWN, LANES).transpose(1, 0, 2).reshape(rows, LANES)
    n_y, n_z = Y_CHIPS, n_curve // Y_CHIPS
    hbm = pl.BlockSpec(memory_space=pltpu.HBM)
    vmem = pl.BlockSpec(memory_space=pltpu.VMEM)
    dma = pltpu.SemaphoreType.DMA
    state = pl.pallas_call(
        functools.partial(exchange_kernel, n_curve, n_near),
        out_shape=(
            pltpu.VMEM((7, 6, ROWS, LANES), F32),
            pltpu.VMEM((6, 6, ROWS, LANES), F32),
            pltpu.VMEM((2, 7, DEPTH, ROWS, LANES), F32),
            pltpu.VMEM((2, 6, DEPTH, ROWS, LANES), F32),
            pltpu.VMEM((1, LANES), F32),
            pltpu.VMEM((2, LANES), F32),
        ),
        in_specs=[hbm] * 3,
        out_specs=(vmem,) * 6,
        scratch_shapes=[
            pltpu.VMEM((7, rows, LANES), F32),
            pltpu.VMEM((7, NEXT, LANES), F32),
            pltpu.VMEM((7, PREV, LANES), F32),
            pltpu.VMEM((7, 8, ROWS, LANES), F32),
            pltpu.VMEM((6, 8, ROWS, LANES), F32),
            pltpu.VMEM((7, 2, ROWS, LANES), F32),
            pltpu.VMEM((7, 2, ROWS, LANES), F32),
            pltpu.VMEM((2, 1, LANES), F32),
            pltpu.VMEM((max(n_near * n_y - 1, 2 * n_z - 1), 1, LANES), F32),
            pltpu.VMEM((n_z, 1, LANES), F32),
            pltpu.VMEM((1, LANES), F32),
            pltpu.VMEM((1, LANES), F32),
            pltpu.SMEM((BOXES,), jnp.int32),
            dma((3,)),
            dma((2,)),
            dma((2,)),
            dma((5,)),
            dma((5,)),
            pltpu.SemaphoreType.REGULAR((2,)),
        ],
        compiler_params=pltpu.CompilerParams(collective_id=0, has_side_effects=True, vmem_limit_bytes=VMEM_LIMIT),
        name="exchange",
    )(*(pltpu.with_memory_space_constraint(v, pltpu.HBM) for v in (prim, cond, new_owner)))
    out = pl.pallas_call(
        finish_kernel,
        out_shape=jax.ShapeDtypeStruct((6, 32 * DEPTH, LANES), F32),
        in_specs=[vmem] * 6,
        out_specs=vmem,
        scratch_shapes=[
            pltpu.VMEM((6, 6, ROWS, LANES), F32),
            pltpu.VMEM((4, 6, ROWS, LANES), F32),
            pltpu.VMEM((6, BOXES + 1, 8, LANES), F32),
        ],
        compiler_params=pltpu.CompilerParams(vmem_limit_bytes=VMEM_LIMIT),
        name="finish",
    )(*(pltpu.with_memory_space_constraint(v, pltpu.VMEM) for v in state))
    out = out.reshape(6, 32, DEPTH, LANES).transpose(0, 2, 1, 3).reshape(6, DEPTH, 32 * LANES)
    return out[None]


def solution(mesh):
    n_curve, n_near = mesh.shape["curve"], mesh.shape["near"]
    return jax.shard_map(
        functools.partial(local, n_curve, n_near),
        mesh=mesh,
        in_specs=(P(None, "near", "curve"), P("near", "curve"), P("curve")),
        out_specs=P("curve", None, "near", None),
        check_vma=False,
    )
```
